128 devices in a mesh: wide: 8 (over y_hi, x), narrow: 16 (over y_lo, z, core).
Axes of the slice: x: 4, y: 4 (y_hi: 2, y_lo: 2; y = y_hi * 2 + y_lo), z: 4, core: 2. Of those that a mesh axis runs over, the one named last changes fastest.
Arguments:
- saved_inputs: bfloat16 [3, 16384, 8192], P(None, 'wide', 'narrow'), may hold values from -6 to 6
- cotangent: bfloat16 [16384, 8192], P('wide', 'narrow'), may hold values from -6 to 6
- w_self: bfloat16 [3, 8192, 512], P(None, 'narrow'), may hold values from -0.1875 to 0.1875
- w_cross: bfloat16 [3, 8192, 512], P(None, 'narrow'), may hold values from -0.1875 to 0.1875
Outputs:
- grad_in: bfloat16 [16384, 8192], P('wide', 'narrow')
- grad_self: float32 [3, 8192, 512], P(None, ('narrow', 'wide'))
- grad_cross: float32 [3, 8192, 512], P(None, ('narrow', 'wide'))
The draws below stay inside these ranges and needn't reach their ends.
All inputs are finite; a program needn't handle non-finite values.
Results may differ from the reference program's by a relative error of at most 0.0057.
Values may be sent and summed in bfloat16 or wider, within the bound.
A program may use at most 128 MiB of HBM per device.

```python
import math
import jax
import jax.numpy as jnp
import numpy as np

BLK = 512
LEVELS = 3
D = 8192
TOKENS = 16384


def spiked(result, stream_key, source, target, parts, factor):
    def block_of(dim):
        return (jnp.arange(result.shape[dim]) // (result.shape[dim] // parts)).reshape((-1,) + (1,) * (result.ndim - 1 - dim))

    one_side = jax.random.permutation(stream_key, parts)[block_of(target)]
    second = (block_of(target) + parts // 2) % parts
    return jnp.where((block_of(source) == one_side) | (block_of(source) == second), factor * result, result)


def block_levels(stream_key, extent, cuts, smallest, top_value):
    level, own = 1.0, jax.random.fold_in(stream_key, 6)
    for position, parts in cuts:
        draws = jnp.exp(jax.random.uniform(jax.random.fold_in(own, position), (parts,), jnp.float32, smallest / len(cuts), top_value / len(cuts)))
        level = level * jnp.repeat(draws, extent[position] // parts).reshape([-1 if axis == position else 1 for axis in range(len(extent))])
    return level


def centred(key, dims, deviation, most, shards=(), dtype=jnp.bfloat16):
    drawn = deviation * jax.random.normal(key, dims, jnp.float32)
    if shards:
        drawn = drawn * block_levels(key, dims, shards, -0.22, 0.18)
    return jnp.clip(drawn, -most, most).astype(dtype)


def bell_draw_with(rng, extent, deviation, limit, shards, heavy, dtype=jnp.bfloat16):
    drawn = deviation * jax.random.normal(rng, extent, jnp.float32)
    if shards:
        drawn = drawn * block_levels(rng, extent, shards, -0.22, 0.18)
    return jnp.clip(spiked(drawn, jax.random.fold_in(rng, 3), *heavy), -limit, limit).astype(dtype)


def setup_inputs(seed: int = 0) -> dict:
    key_of = jax.random.split(jax.random.key(seed), 5)
    saved_inputs = bell_draw_with(key_of[0], (LEVELS, TOKENS, D), 1.0, 6.0, ((1, 8), (2, 16)), (1, 2, 16, 2.0))
    cotangent = centred(key_of[1], (TOKENS, D), 1.0, 6.0, ((0, 8), (1, 16)))
    w_self = centred(key_of[2], (LEVELS, D, BLK), (2 * BLK) ** -0.5, 0.1875, ((1, 16),))
    w_cross = centred(key_of[3], (LEVELS, D, BLK), (2 * BLK) ** -0.5, 0.1875, ((1, 16),))
    return dict(saved_inputs=saved_inputs, cotangent=cotangent, w_self=w_self, w_cross=w_cross)


def reference(saved_inputs, cotangent, w_self, w_cross):
    blocks = D // BLK
    scale = 1.0 / math.sqrt(TOKENS)
    grad = cotangent.reshape(TOKENS, blocks, BLK)
    self_list = [None] * LEVELS
    cross_list = [None] * LEVELS
    for level in reversed(range(LEVELS)):
        partner = np.arange(blocks) ^ 1 << level
        inputs = saved_inputs[level].reshape(TOKENS, blocks, BLK).astype(jnp.float32)
        gflt = grad.astype(jnp.float32)
        a_blocks = w_self[level].reshape(blocks, BLK, BLK).astype(jnp.float32)
        c_blocks = w_cross[level].reshape(blocks, BLK, BLK).astype(jnp.float32)
        self_list[level] = (jnp.einsum('tnk,tnj->nkj', inputs, gflt) * scale).reshape(D, BLK)
        cross_list[level] = (jnp.einsum('tnk,tnj->nkj', inputs[:, partner], gflt) * scale).reshape(D, BLK)
        own = jnp.einsum('tnj,nkj->tnk', gflt, a_blocks)
        far = jnp.einsum('tnj,nkj->tnk', gflt[:, partner], c_blocks[partner])
        grad = (own + far).astype(jnp.bfloat16)
    return (grad.reshape(TOKENS, D), jnp.stack(self_list), jnp.stack(cross_list))
```

```python
import math

import jax
import jax.numpy as jnp
from jax import lax
from jax.experimental import pallas as pl
from jax.experimental.pallas import tpu as pltpu
from jax.sharding import PartitionSpec as P

LEVELS = 3
NC = 4
WX = 4
MESH = pl.DeviceIdType.MESH

C2_P, A2_Q, C2_R, A2_P, C1_Q = range(5)
SELF2, CROSS2, SELF1, CROSS1, CROSS0, SELF0 = range(6)


def flip(n, bit):
    return n + bit - 2 * bit * lax.rem(lax.div(n, bit), 2)


def outer(left, right):
    return lax.dot_general(left, right, (((0,), (0,)), ((), ())), preferred_element_type=jnp.float32)


def trans(left, right):
    return lax.dot_general(left, right, (((1,), (1,)), ((), ())), preferred_element_type=jnp.float32)


def kernel(
    wide, scale,
    x_hbm, g_hbm, ws_hbm, wc_hbm,
    out_hbm, gs_hbm, gc_hbm,
    xv, g2, av, cv, far, far0, rq, rr, part, g1z, g1q, help1, g0z, g0o, outv,
    acc, sb, rb, res, cres,
    ld, push_s, push_r, bc_s, bc_r, c0_s, c0_r, h1_s, h1_r, h2_s, h2_r,
    l1_s, l1_r, l0_s, l0_r, rs_s, rs_r, cr_s, cr_r, wr,
):
    w = lax.axis_index("wide")
    n = lax.axis_index("narrow")
    wx, wy = lax.rem(w, WX), lax.div(w, WX)
    peers = []
    for dy in range(wide // WX):
        for dx in (1, 3, 2, 0):
            if dx or dy:
                peers.append(lax.rem(wy + dy, wide // WX) * WX + lax.rem(wx + dx, WX))
    q, r, p, co = flip(n, 2), flip(flip(n, 2), 4), flip(n, 4), flip(n, 1)
    half = g2.shape[1]
    ch = half // NC
    blk = g2.shape[2]
    rows = blk // wide
    h = lax.rem(lax.div(n, 4), 2)
    off_h = pl.multiple_of(h * half, half)
    off_o = pl.multiple_of((1 - h) * half, half)
    mine = pl.ds(pl.multiple_of(w * rows, rows), rows)

    def cut(k):
        return pl.ds(pl.multiple_of(k * ch, ch), ch)

    loads = {}

    def load(name, i, src, dst):
        c = pltpu.make_async_copy(src, dst, ld.at[i])
        c.start()
        loads[name] = c

    load("gh", 0, g_hbm.at[pl.ds(off_h, half)], g2.at[0])
    load("go", 1, g_hbm.at[pl.ds(off_o, half)], g2.at[1])
    load("x2h", 2, x_hbm.at[2, pl.ds(off_h, half)], xv.at[2, 0])
    load("x2o", 3, x_hbm.at[2, pl.ds(off_o, half)], xv.at[2, 1])
    load("a", 4, ws_hbm, av)
    load("c", 5, wc_hbm, cv)
    load("x1h", 6, x_hbm.at[1, pl.ds(off_h, half)], xv.at[1, 0])
    load("x1o", 7, x_hbm.at[1, pl.ds(off_o, half)], xv.at[1, 1])
    load("x0h", 8, x_hbm.at[0, pl.ds(off_h, half)], xv.at[0, 0])
    load("x0o", 9, x_hbm.at[0, pl.ds(off_o, half)], xv.at[0, 1])

    barrier = pltpu.get_barrier_semaphore()
    for other in [(w, q), (w, r), (w, p), (w, co)] + [(v, n) for v in peers]:
        pl.semaphore_signal(barrier, inc=1, device_id=other, device_id_type=MESH)
    pl.semaphore_wait(barrier, 4 + len(peers))

    def remote(src, dst, send, recv, to):
        return pltpu.make_async_remote_copy(
            src_ref=src, dst_ref=dst, send_sem=send, recv_sem=recv, device_id=to, device_id_type=MESH
        )

    pushes = []
    for i, (src, level, to) in enumerate(
        ((wc_hbm, 2, p), (ws_hbm, 2, q), (wc_hbm, 2, r), (ws_hbm, 2, p), (wc_hbm, 1, q))
    ):
        c = remote(src.at[level, mine], far.at[i, mine], push_s.at[i], push_r.at[i], (w, to))
        c.start()
        pushes.append(c)
    c0 = remote(wc_hbm.at[0], far0, c0_s, c0_r, (w, co))
    c0.start()

    def hop1(k):
        j = lax.rem(k + NC // 2, NC)
        to_q = remote(g_hbm.at[pl.ds(pl.multiple_of(off_h + k * ch, ch), ch)], rq.at[cut(k)], h1_s.at[0, k], h1_r.at[0, k], (w, q))
        to_r = remote(g_hbm.at[pl.ds(pl.multiple_of(off_o + j * ch, ch), ch)], rr.at[cut(j)], h1_s.at[1, j], h1_r.at[1, j], (w, r))
        return to_q, to_r

    def hop2(k):
        j = lax.rem(k + NC // 2, NC)
        to_r = remote(rq.at[cut(k)], part.at[1, cut(k)], h2_s.at[1, k], h2_r.at[1, k], (w, r))
        to_q = remote(rr.at[cut(j)], part.at[0, cut(j)], h2_s.at[0, j], h2_r.at[0, j], (w, q))
        return to_r, to_q

    @pl.loop(0, NC)
    def _(k):
        to_q, to_r = hop1(k)
        to_q.start()
        to_r.start()

    def scatter(t):
        for d, v in enumerate(peers):
            there = pl.ds(pl.multiple_of(v * rows, rows), rows)
            remote(sb.at[t, there], rb.at[t, d], rs_s.at[t], rs_r.at[t], (v, n)).start()

    def pack(t):
        sb[t] = acc[t].astype(jnp.bfloat16)

    for name in ("gh", "go", "x2h", "x2o"):
        loads[name].wait()
    for s in range(2):
        d = outer(xv[2, s], g2[s])
        if s == 0:
            acc[SELF2] = d
        else:
            acc[SELF2] += d
    pack(SELF2)

    @pl.loop(0, 5)
    def _(i):
        pltpu.make_async_copy(far.at[i, pl.ds(0, rows)], far.at[i, pl.ds(0, rows)], push_r.at[i]).wait()
        for v in peers:
            remote(far.at[i, mine], far.at[i, mine], bc_s.at[i], bc_r.at[i], (v, n)).start()

    scatter(SELF2)

    def gathered(i):
        all7 = pl.ds(0, rows * len(peers))
        pltpu.make_async_copy(far.at[i, all7], far.at[i, all7], bc_r.at[i]).wait()

    for t in (CROSS2, SELF1, CROSS1, CROSS0, SELF0):
        acc[t] = jnp.zeros((blk, blk), jnp.float32)

    @pl.loop(0, NC)
    def _(k):
        to_q, to_r = hop1(k)
        to_r2, to_q2 = hop2(k)
        to_q.wait_recv()
        to_r2.start()
        to_r.wait_recv()
        to_q2.start()

    for name in ("a", "c", "x1h", "x1o", "x0h", "x0o"):
        loads[name].wait()
    for i in range(5):
        gathered(i)
    c0.wait_recv()

    @pl.loop(0, NC)
    def _(k):
        s = cut(k)
        y = trans(rq[s], far[A2_Q]) + trans(rr[s], far[C2_R])
        g1q[0, s] = y.astype(jnp.bfloat16)

    def level2(side, k):
        s = cut(k)
        g = part[side, s]
        acc[CROSS2] += outer(xv[2, side, s], g)
        y = trans(g2[side, s], av[2]) + trans(g, far[C2_P])
        y = y.astype(jnp.bfloat16)
        g1z[side, s] = y
        acc[SELF1] += outer(xv[1, side, s], y)

    def level0_send(side, k):
        s = cut(k)
        return remote(g0z.at[side, s], g0o.at[side, s], l0_s.at[side, k], l0_r.at[side, k], (w, co))

    def level1(side, k):
        s = cut(k)
        g = g1q[side, s]
        acc[CROSS1] += outer(xv[1, side, s], g)
        y = trans(g1z[side, s], av[1]) + trans(g, far[C1_Q])
        g0z[side, s] = y.astype(jnp.bfloat16)

    def level0(side, k):
        s = cut(k)
        y = g0z[side, s]
        acc[SELF0] += outer(xv[0, side, s], y)
        level0_send(side, k).wait_recv()
        g = g0o[side, s]
        acc[CROSS0] += outer(xv[0, side, s], g)
        outv[side, s] = (trans(y, av[0]) + trans(g, far0[...])).astype(jnp.bfloat16)

    def level1_sends(k):
        s = cut(k)
        to_q = remote(g1z.at[1, s], g1q.at[1, s], l1_s.at[0, k], l1_r.at[0, k], (w, q))
        to_r = remote(help1.at[s], g1q.at[1, cut(k + NC // 2)], l1_s.at[1, k], l1_r.at[1, k], (w, r))
        return to_q, to_r

    @pl.loop(0, NC)
    def _(k):
        j = lax.rem(k + NC // 2, NC)
        _, to_q2 = hop2(k)
        to_r2, _ = hop2(k)
        to_q2.wait_recv()
        to_r2.wait_recv()

        @pl.when(k < NC // 2)
        def _():
            s = cut(j)
            y = trans(part[0, s], far[A2_P]) + trans(g2[0, s], cv[2])
            help1[cut(k)] = y.astype(jnp.bfloat16)

        level2(1, k)
        level2(0, j)

        @pl.when(k < NC // 2)
        def _():
            to_q, to_r = level1_sends(k)
            to_q.start()
            to_r.start()

        level1(0, j)
        level0_send(0, j).start()

    pack(CROSS2)
    pack(SELF1)

    @pl.loop(0, NC)
    def _(k):
        level0(0, lax.rem(k + NC // 2, NC))

        @pl.when(k == 0)
        def _():
            scatter(CROSS2)
            scatter(SELF1)

    @pl.loop(0, NC // 2)
    def _(k):
        to_q, to_r = level1_sends(k)
        to_q.wait_recv()
        level1(1, k)
        to_r.wait_recv()
        level1(1, k + NC // 2)
        level0_send(1, k).start()
        level0_send(1, k + NC // 2).start()

    pack(CROSS1)

    @pl.loop(0, NC)
    def _(k):
        level0(1, k)

        @pl.when(k == 0)
        def _():
            scatter(CROSS1)

    pack(CROSS0)
    pack(SELF0)
    writes = []
    for s, off in ((0, off_h), (1, off_o)):
        c = pltpu.make_async_copy(outv.at[s], out_hbm.at[pl.ds(off, half)], wr.at[s])
        c.start()
        writes.append(c)
    scatter(CROSS0)
    scatter(SELF0)

    level_of = {SELF2: 2, CROSS2: 2, SELF1: 1, CROSS1: 1, CROSS0: 0, SELF0: 0}
    cross_backs = []
    for t in (SELF2, CROSS2, SELF1, CROSS1, CROSS0, SELF0):
        pltpu.make_async_copy(rb.at[t], rb.at[t], rs_r.at[t]).wait()
        total = acc[t, mine]
        for d in range(len(peers)):
            total = total + rb[t, d].astype(jnp.float32)
        res[t] = total * scale
        level = level_of[t]
        if t in (SELF2, SELF1, SELF0):
            c = pltpu.make_async_copy(res.at[t], gs_hbm.at[level], wr.at[2 + level])
            c.start()
            writes.append(c)
        else:
            c = remote(res.at[t], cres.at[level], cr_s.at[level], cr_r.at[level], (w, flip(n, 1 << level)))
            c.start()
            cross_backs.append((level, c))
    for level, c in cross_backs:
        c.wait()
        o = pltpu.make_async_copy(cres.at[level], gc_hbm.at[level], wr.at[5 + level])
        o.start()
        writes.append(o)

    for c in pushes:
        c.wait_send()
    c0.wait_send()

    @pl.loop(0, NC)
    def _(k):
        for c in hop1(k) + hop2(k) + (level0_send(0, k), level0_send(1, k)):
            c.wait_send()

    @pl.loop(0, NC // 2)
    def _(k):
        for c in level1_sends(k):
            c.wait_send()

    for i in range(5):
        all7 = pl.ds(0, rows * len(peers))
        pltpu.make_async_copy(far.at[i, all7], far.at[i, all7], bc_s.at[i]).wait()
    for t in range(6):
        pltpu.make_async_copy(rb.at[t], rb.at[t], rs_s.at[t]).wait()
    for c in writes:
        c.wait()


def local(saved_inputs, cotangent, w_self, w_cross):
    wide = lax.axis_size("wide")
    tokens, blk = cotangent.shape
    scale = 1.0 / math.sqrt(tokens * wide)
    half, rows = tokens // 2, blk // wide
    bf, f32 = jnp.bfloat16, jnp.float32
    dma = pltpu.SemaphoreType.DMA
    both = pltpu.VMEM((2, half, blk), bf)
    square3 = pltpu.VMEM((3, blk, blk), bf)

    def body(*refs):
        kernel(wide, scale, *refs)

    return pl.pallas_call(
        body,
        out_shape=(
            jax.ShapeDtypeStruct((tokens, blk), bf),
            jax.ShapeDtypeStruct((LEVELS, rows, blk), f32),
            jax.ShapeDtypeStruct((LEVELS, rows, blk), f32),
        ),
        in_specs=[pl.BlockSpec(memory_space=pl.ANY)] * 4,
        out_specs=[pl.BlockSpec(memory_space=pl.ANY)] * 3,
        scratch_shapes=[
            pltpu.VMEM((3, 2, half, blk), bf),
            both,
            square3, square3,
            pltpu.VMEM((5, blk, blk), bf),
            pltpu.VMEM((blk, blk), bf),
            pltpu.VMEM((half, blk), bf), pltpu.VMEM((half, blk), bf),
            both, both, both,
            pltpu.VMEM((half // 2, blk), bf),
            both, both, both,
            pltpu.VMEM((6, blk, blk), f32),
            pltpu.VMEM((6, blk, blk), bf),
            pltpu.VMEM((6, wide - 1, rows, blk), bf),
            pltpu.VMEM((6, rows, blk), f32),
            pltpu.VMEM((3, rows, blk), f32),
            dma((10,)),
            dma((5,)), dma((5,)), dma((5,)), dma((5,)),
            dma(()), dma(()),
            dma((2, NC)), dma((2, NC)), dma((2, NC)), dma((2, NC)),
            dma((2, NC // 2)), dma((2, NC // 2)),
            dma((2, NC)), dma((2, NC)),
            dma((6,)), dma((6,)),
            dma((3,)), dma((3,)),
            dma((8,)),
        ],
        compiler_params=pltpu.CompilerParams(
            collective_id=0, has_side_effects=True, vmem_limit_bytes=60 << 20
        ),
        name="butterfly_backward",
    )(saved_inputs, cotangent, w_self, w_cross)


def solution(mesh):
    in_specs = (
        P(None, "wide", "narrow"),
        P("wide", "narrow"),
        P(None, "narrow", None),
        P(None, "narrow", None),
    )
    out_specs = (
        P("wide", "narrow"),
        P(None, ("narrow", "wide"), None),
        P(None, ("narrow", "wide"), None),
    )
    return jax.shard_map(local, mesh=mesh, in_specs=in_specs, out_specs=out_specs, check_vma=False)
```

```python
import math

import jax
import jax.numpy as jnp
from jax import lax
from jax.experimental import pallas as pl
from jax.experimental.pallas import tpu as pltpu
from jax.sharding import PartitionSpec as P

LEVELS = 3
NC = 4
WX = 4
MESH = pl.DeviceIdType.MESH

C2_P, A2_Q, C2_R, A2_P, C1_Q = range(5)
SELF2, CROSS2, SELF1, CROSS1, CROSS0, SELF0 = range(6)


def flip(n, bit):
    return n + bit - 2 * bit * lax.rem(lax.div(n, bit), 2)


def outer(left, right):
    return lax.dot_general(left, right, (((0,), (0,)), ((), ())), preferred_element_type=jnp.float32)


def trans(left, right):
    return lax.dot_general(left, right, (((1,), (1,)), ((), ())), preferred_element_type=jnp.float32)


def remote(src, dst, send, recv, to):
    return pltpu.make_async_remote_copy(
        src_ref=src, dst_ref=dst, send_sem=send, recv_sem=recv, device_id=to, device_id_type=MESH
    )


def wait_for(ref, sem):
    pltpu.make_async_copy(ref, ref, sem).wait()


def kernel(
    wide, scale,
    x_hbm, g_hbm, ws_hbm, wc_hbm,
    outv, gsv, gcv,
    xv, g2, av, cv, far, far0, rq, rr, part, g1z, g1q, help1, g0z, g0o,
    acc, sb, rb, res,
    ld, push_s, push_r, bc_s, bc_r, c0_s, c0_r, h1_s, h1_r, h2_s, h2_r,
    l1_s, l1_r, l0_s, l0_r, rs_s, rs_r, cr_s, cr_r,
):
    w = lax.axis_index("wide")
    n = lax.axis_index("narrow")
    wx, wy = lax.rem(w, WX), lax.div(w, WX)
    peers = []
    for dy in range(wide // WX):
        for dx in (1, 3, 2, 0):
            if dx or dy:
                peers.append(lax.rem(wy + dy, wide // WX) * WX + lax.rem(wx + dx, WX))
    q, r, p, co = flip(n, 2), flip(flip(n, 2), 4), flip(n, 4), flip(n, 1)
    half = g2.shape[1]
    ch = half // NC
    blk = g2.shape[2]
    rows = blk // wide
    h = lax.rem(lax.div(n, 4), 2)
    off_h = pl.multiple_of(h * half, half)
    off_o = pl.multiple_of((1 - h) * half, half)
    mine = pl.ds(pl.multiple_of(w * rows, rows), rows)

    def cut(k):
        return pl.ds(pl.multiple_of(k * ch, ch), ch)

    loads = {}

    def load(name, i, src, dst):
        c = pltpu.make_async_copy(src, dst, ld.at[i])
        c.start()
        loads[name] = c

    load("gh", 0, g_hbm.at[pl.ds(off_h, half)], g2.at[0])
    load("go", 1, g_hbm.at[pl.ds(off_o, half)], g2.at[1])
    load("x2h", 2, x_hbm.at[2, pl.ds(off_h, half)], xv.at[2, 0])
    load("x2o", 3, x_hbm.at[2, pl.ds(off_o, half)], xv.at[2, 1])
    load("a", 4, ws_hbm, av)
    load("c", 5, wc_hbm, cv)
    load("x1h", 6, x_hbm.at[1, pl.ds(off_h, half)], xv.at[1, 0])
    load("x1o", 7, x_hbm.at[1, pl.ds(off_o, half)], xv.at[1, 1])
    load("x0h", 8, x_hbm.at[0, pl.ds(off_h, half)], xv.at[0, 0])
    load("x0o", 9, x_hbm.at[0, pl.ds(off_o, half)], xv.at[0, 1])

    barrier = pltpu.get_barrier_semaphore()
    for other in [(w, q), (w, r), (w, p), (w, co)] + [(v, n) for v in peers]:
        pl.semaphore_signal(barrier, inc=1, device_id=other, device_id_type=MESH)
    pl.semaphore_wait(barrier, 4 + len(peers))

    def push(i, src, to):
        return remote(src, far.at[i, mine], push_s.at[i], push_r.at[i], (w, to))

    def first_pushes():
        return (
            push(C2_R, wc_hbm.at[2, mine], r),
            push(A2_Q, ws_hbm.at[2, mine], q),
            push(C1_Q, wc_hbm.at[1, mine], q),
        )

    def second_pushes():
        return push(C2_P, far.at[C2_R, mine], q), push(A2_P, far.at[A2_Q, mine], r)

    def h_at(k):
        return lax.rem(2 * k + 1, NC) - lax.div(k, 2)

    def o_at(k):
        return lax.rem(2 * k, NC) + lax.div(k, 2)

    def hop1(k):
        i, j = o_at(k), h_at(k)
        to_q = remote(g_hbm.at[pl.ds(pl.multiple_of(off_h + i * ch, ch), ch)], rq.at[cut(i)], h1_s.at[0, i], h1_r.at[0, i], (w, q))
        to_r = remote(g_hbm.at[pl.ds(pl.multiple_of(off_o + j * ch, ch), ch)], rr.at[cut(j)], h1_s.at[1, j], h1_r.at[1, j], (w, r))
        return to_q, to_r

    def hop2(k):
        i, j = o_at(k), h_at(k)
        to_r = remote(rq.at[cut(i)], part.at[1, cut(i)], h2_s.at[1, i], h2_r.at[1, i], (w, r))
        to_q = remote(rr.at[cut(j)], part.at[0, cut(j)], h2_s.at[0, j], h2_r.at[0, j], (w, q))
        return to_r, to_q

    def start(copies):
        for c in copies:
            c.start()

    start(first_pushes())
    start(hop1(0))
    c0 = remote(wc_hbm.at[0], far0, c0_s, c0_r, (w, co))
    c0.start()

    def arrived(i):
        wait_for(far.at[i, mine], push_r.at[i])

    arrived(C2_R)
    arrived(A2_Q)
    start(second_pushes())

    @pl.loop(1, NC)
    def _(k):
        start(hop1(k))

    def spread(i):
        for v in peers:
            remote(far.at[i, mine], far.at[i, mine], bc_s.at[i], bc_r.at[i], (v, n)).start()

    spread(C2_R)
    spread(A2_Q)

    def scatter(t):
        for d, v in enumerate(peers):
            there = pl.ds(pl.multiple_of(v * rows, rows), rows)
            remote(sb.at[t, there], rb.at[t, d], rs_s.at[t], rs_r.at[t], (v, n)).start()

    def pack(t):
        sb[t] = acc[t].astype(jnp.bfloat16)

    for name in ("gh", "go", "x2h", "x2o"):
        loads[name].wait()
    for s in range(2):
        d = outer(xv[2, s], g2[s])
        if s == 0:
            acc[SELF2] = d
        else:
            acc[SELF2] += d
    pack(SELF2)

    for i in (C2_P, A2_P, C1_Q):
        arrived(i)
        spread(i)
    scatter(SELF2)

    def gathered(i):
        all7 = pl.ds(0, rows * len(peers))
        wait_for(far.at[i, all7], bc_r.at[i])

    for t in (CROSS2, SELF1, CROSS1, CROSS0, SELF0):
        acc[t] = jnp.zeros((blk, blk), jnp.float32)

    @pl.loop(0, NC)
    def _(k):
        to_q, to_r = hop1(k)
        to_r2, to_q2 = hop2(k)
        to_q.wait_recv()
        to_r2.start()
        to_r.wait_recv()
        to_q2.start()

    for name in ("a", "c", "x1h", "x1o", "x0h", "x0o"):
        loads[name].wait()
    for i in range(5):
        gathered(i)
    c0.wait_recv()

    @pl.loop(0, NC)
    def _(k):
        s = cut(k)
        y = trans(rq[s], far[A2_Q]) + trans(rr[s], far[C2_R])
        g1q[0, s] = y.astype(jnp.bfloat16)

    def level2(side, k):
        s = cut(k)
        g = part[side, s]
        acc[CROSS2] += outer(xv[2, side, s], g)
        y = trans(g2[side, s], av[2]) + trans(g, far[C2_P])
        y = y.astype(jnp.bfloat16)
        g1z[side, s] = y
        acc[SELF1] += outer(xv[1, side, s], y)

    def level0_send(side, k):
        s = cut(k)
        return remote(g0z.at[side, s], g0o.at[side, s], l0_s.at[side, k], l0_r.at[side, k], (w, co))

    def level1(side, k):
        s = cut(k)
        y = trans(g1z[side, s], av[1]) + trans(g1q[side, s], far[C1_Q])
        g0z[side, s] = y.astype(jnp.bfloat16)

    def pair(k):
        return pl.ds(pl.multiple_of(2 * k * ch, 2 * ch), 2 * ch)

    def add(t, level, side, s, g):
        acc[t] += outer(xv[level, side, s], g[side, s])

    def last(side, s):
        y = trans(g0z[side, s], av[0]) + trans(g0o[side, s], far0[...])
        outv[side, s] = y.astype(jnp.bfloat16)

    def level1_sends(k):
        to_q = remote(g1z.at[1, cut(2 * k)], g1q.at[1, cut(2 * k)], l1_s.at[0, k], l1_r.at[0, k], (w, q))
        to_r = remote(help1.at[cut(k)], g1q.at[1, cut(2 * k + 1)], l1_s.at[1, k], l1_r.at[1, k], (w, r))
        return to_q, to_r

    @pl.loop(0, NC)
    def _(k):
        i, j = o_at(k), h_at(k)
        to_r2, to_q2 = hop2(k)
        to_q2.wait_recv()

        @pl.when(k < NC // 2)
        def _():
            s = cut(j)
            y = trans(part[0, s], far[A2_P]) + trans(g2[0, s], cv[2])
            help1[cut(k)] = y.astype(jnp.bfloat16)

        to_r2.wait_recv()
        level2(1, i)

        @pl.when(k < NC // 2)
        def _():
            start(level1_sends(k))

        level2(0, j)

        @pl.when(k == NC - 1)
        def _():
            pack(CROSS2)
            pack(SELF1)

        level1(0, j)

        @pl.when(k == NC - 1)
        def _():
            scatter(CROSS2)
            scatter(SELF1)

        level0_send(0, j).start()

    @pl.loop(0, NC // 2)
    def _(k):
        s = pair(k)
        add(CROSS1, 1, 0, s, g1q)
        add(SELF0, 0, 0, s, g0z)
        level0_send(0, 2 * k).wait_recv()
        level0_send(0, 2 * k + 1).wait_recv()
        add(CROSS0, 0, 0, s, g0o)
        last(0, s)

    @pl.loop(0, NC // 2)
    def _(k):
        s = pair(k)
        to_q, to_r = level1_sends(k)
        to_q.wait_recv()
        level1(1, 2 * k)
        to_r.wait_recv()
        level1(1, 2 * k + 1)
        level0_send(1, 2 * k).start()
        add(CROSS1, 1, 1, s, g1q)
        level0_send(1, 2 * k + 1).start()

        @pl.when(k == NC // 2 - 1)
        def _():
            pack(CROSS1)

        add(SELF0, 0, 1, s, g0z)

        @pl.when(k == NC // 2 - 1)
        def _():
            scatter(CROSS1)

        level0_send(1, 2 * k).wait_recv()
        level0_send(1, 2 * k + 1).wait_recv()
        add(CROSS0, 0, 1, s, g0o)

        @pl.when(k == NC // 2 - 1)
        def _():
            pack(CROSS0)
            pack(SELF0)
            scatter(CROSS0)
            scatter(SELF0)

        last(1, s)

    level_of = {SELF2: 2, CROSS2: 2, SELF1: 1, CROSS1: 1, CROSS0: 0, SELF0: 0}
    cross_backs = []
    for t in (SELF2, CROSS2, SELF1, CROSS1, CROSS0, SELF0):
        wait_for(rb.at[t], rs_r.at[t])
        total = acc[t, mine]
        for d in range(len(peers)):
            total = total + rb[t, d].astype(jnp.float32)
        total = total * scale
        level = level_of[t]
        if t in (SELF2, SELF1, SELF0):
            gsv[level] = total
        else:
            res[level] = total
            c = remote(res.at[level], gcv.at[level], cr_s.at[level], cr_r.at[level], (w, flip(n, 1 << level)))
            cross_backs.append(c)
            c.start()
    for c in cross_backs:
        c.wait()

    for c in first_pushes() + second_pushes():
        c.wait_send()
    c0.wait_send()

    @pl.loop(0, NC)
    def _(k):
        for c in hop1(k) + hop2(k) + (level0_send(0, k), level0_send(1, k)):
            c.wait_send()

    @pl.loop(0, NC // 2)
    def _(k):
        for c in level1_sends(k):
            c.wait_send()

    for i in range(5):
        all7 = pl.ds(0, rows * len(peers))
        wait_for(far.at[i, all7], bc_s.at[i])
    for t in range(6):
        wait_for(rb.at[t], rs_s.at[t])


def write_out(outv, gsv, gcv, out_hbm, gs_hbm, gc_hbm, sem):
    n = lax.axis_index("narrow")
    half = outv.shape[1]
    h = lax.rem(lax.div(n, 4), 2)
    copies = []
    for i, (src, dst) in enumerate((
        (outv.at[0], out_hbm.at[pl.ds(pl.multiple_of(h * half, half), half)]),
        (outv.at[1], out_hbm.at[pl.ds(pl.multiple_of((1 - h) * half, half), half)]),
        (gsv, gs_hbm),
        (gcv, gc_hbm),
    )):
        c = pltpu.make_async_copy(src, dst, sem.at[i])
        c.start()
        copies.append(c)
    for c in copies:
        c.wait()


def local(saved_inputs, cotangent, w_self, w_cross):
    wide = lax.axis_size("wide")
    tokens, blk = cotangent.shape
    scale = 1.0 / math.sqrt(tokens * wide)
    half, rows = tokens // 2, blk // wide
    bf, f32 = jnp.bfloat16, jnp.float32
    dma = pltpu.SemaphoreType.DMA
    both = pltpu.VMEM((2, half, blk), bf)
    square3 = pltpu.VMEM((3, blk, blk), bf)

    def body(*refs):
        kernel(wide, scale, *refs)

    vmem, anywhere = pl.BlockSpec(memory_space=pltpu.VMEM), pl.BlockSpec(memory_space=pl.ANY)
    kept = pl.pallas_call(
        body,
        out_shape=(
            pltpu.VMEM((2, half, blk), bf),
            pltpu.VMEM((LEVELS, rows, blk), f32),
            pltpu.VMEM((LEVELS, rows, blk), f32),
        ),
        in_specs=[anywhere] * 4,
        out_specs=[vmem] * 3,
        scratch_shapes=[
            pltpu.VMEM((3, 2, half, blk), bf),
            both,
            square3, square3,
            pltpu.VMEM((5, blk, blk), bf),
            pltpu.VMEM((blk, blk), bf),
            pltpu.VMEM((half, blk), bf), pltpu.VMEM((half, blk), bf),
            both, both, both,
            pltpu.VMEM((half // 2, blk), bf),
            both, both,
            pltpu.VMEM((6, blk, blk), f32),
            pltpu.VMEM((6, blk, blk), bf),
            pltpu.VMEM((6, wide - 1, rows, blk), bf),
            pltpu.VMEM((3, rows, blk), f32),
            dma((10,)),
            dma((5,)), dma((5,)), dma((5,)), dma((5,)),
            dma(()), dma(()),
            dma((2, NC)), dma((2, NC)), dma((2, NC)), dma((2, NC)),
            dma((2, NC // 2)), dma((2, NC // 2)),
            dma((2, NC)), dma((2, NC)),
            dma((6,)), dma((6,)),
            dma((3,)), dma((3,)),
        ],
        compiler_params=pltpu.CompilerParams(
            collective_id=0, has_side_effects=True, vmem_limit_bytes=60 << 20
        ),
        name="butterfly_backward",
    )(saved_inputs, cotangent, w_self, w_cross)
    return pl.pallas_call(
        write_out,
        out_shape=(
            jax.ShapeDtypeStruct((tokens, blk), bf),
            jax.ShapeDtypeStruct((LEVELS, rows, blk), f32),
            jax.ShapeDtypeStruct((LEVELS, rows, blk), f32),
        ),
        in_specs=[vmem] * 3,
        out_specs=[anywhere] * 3,
        scratch_shapes=[dma((4,))],
        compiler_params=pltpu.CompilerParams(vmem_limit_bytes=8 << 20),
        name="write_out",
    )(*kept)


def solution(mesh):
    in_specs = (
        P(None, "wide", "narrow"),
        P("wide", "narrow"),
        P(None, "narrow", None),
        P(None, "narrow", None),
    )
    out_specs = (
        P("wide", "narrow"),
        P(None, ("narrow", "wide"), None),
        P(None, ("narrow", "wide"), None),
    )
    return jax.shard_map(local, mesh=mesh, in_specs=in_specs, out_specs=out_specs, check_vma=False)
```

```python
import math

import jax
import jax.numpy as jnp
from jax import lax
from jax.experimental import pallas as pl
from jax.experimental.pallas import tpu as pltpu
from jax.sharding import PartitionSpec as P

LEVELS = 3
NC = 4
WX = 4
MESH = pl.DeviceIdType.MESH

C2_P, A2_Q, C2_R, A2_P, C1_Q = range(5)
SELF2, CROSS2, SELF1, CROSS1, CROSS0, SELF0 = range(6)


def flip(n, bit):
    return n + bit - 2 * bit * lax.rem(lax.div(n, bit), 2)


def outer(left, right):
    return lax.dot_general(left, right, (((0,), (0,)), ((), ())), preferred_element_type=jnp.float32)


def trans(left, right):
    return lax.dot_general(left, right, (((1,), (1,)), ((), ())), preferred_element_type=jnp.float32)


def remote(src, dst, send, recv, to):
    return pltpu.make_async_remote_copy(
        src_ref=src, dst_ref=dst, send_sem=send, recv_sem=recv, device_id=to, device_id_type=MESH
    )


def wait_for(ref, sem):
    pltpu.make_async_copy(ref, ref, sem).wait()


def kernel(
    wide, scale,
    x_hbm, g_hbm, ws_hbm, wc_hbm,
    outv, gsv, gcv,
    xv, g2, av, cv, far, far0, rq, rr, part, g1z, g1q, help1, g0z, g0o,
    acc, sb, got_own, got_x, got_y, sum_x, sum_y, own_x, own_y, end_y, end_x, res,
    ld, push_s, push_r, wy1_s, wy1_r, wx1_s, wx1_r, wx2_s, wx2_r, wy2_s, wy2_r, c0_s, c0_r, h1_s, h1_r, h2_s, h2_r,
    l1_s, l1_r, l0_s, l0_r, sx1_s, sx1_r, sy1_s, sy1_r, sy2_s, sy2_r, sx2_s, sx2_r, cr_s, cr_r, co_s, co_r,
):
    w = lax.axis_index("wide")
    n = lax.axis_index("narrow")
    wx, wy = lax.rem(w, WX), lax.div(w, WX)
    oy = 1 - wy
    x_peers = [lax.rem(wx + dx, WX) for dx in (1, 3, 2)]
    q, r, p, co = flip(n, 2), flip(flip(n, 2), 4), flip(n, 4), flip(n, 1)
    half = g2.shape[1]
    ch = half // NC
    blk = g2.shape[2]
    rows = blk // wide
    cols = blk // 2
    left, right = pl.ds(0, cols), pl.ds(cols, cols)
    beside_x = [(wy * WX + v, n) for v in x_peers]
    beside_y = (oy * WX + wx, n)
    across_x = [(v, co) for v, _ in beside_x]
    across_y = (oy * WX + wx, co)
    h = lax.rem(lax.div(n, 4), 2)
    off_h = pl.multiple_of(h * half, half)
    off_o = pl.multiple_of((1 - h) * half, half)
    mine = pl.ds(pl.multiple_of(w * rows, rows), rows)

    def rows_of(y, x, many=1):
        return pl.ds(pl.multiple_of((y * WX + x) * rows, rows), many * rows)

    def cut(k):
        return pl.ds(pl.multiple_of(k * ch, ch), ch)

    loads = {}

    def load(name, i, src, dst):
        c = pltpu.make_async_copy(src, dst, ld.at[i])
        c.start()
        loads[name] = c

    barrier = pltpu.get_barrier_semaphore()
    for other in [(w, q), (w, r), (w, p), (w, co), beside_y, across_y] + beside_x + across_x:
        pl.semaphore_signal(barrier, inc=1, device_id=other, device_id_type=MESH)
    pl.semaphore_wait(barrier, 6 + 2 * len(beside_x))

    def push(i, src, to):
        return remote(src, far.at[i, wy, wx], push_s.at[i], push_r.at[i], (w, to))

    def first_pushes():
        return (
            push(C2_R, wc_hbm.at[2, mine], r),
            push(A2_Q, ws_hbm.at[2, mine], q),
            push(C1_Q, wc_hbm.at[1, mine], q),
        )

    def second_pushes():
        return push(C2_P, far.at[C2_R, wy, wx], q), push(A2_P, far.at[A2_Q, wy, wx], r)

    def h_at(k):
        return lax.rem(2 * k, NC) + 1 - lax.div(k, NC // 2)

    def o_at(k):
        return lax.rem(2 * k, NC) + lax.div(k, NC // 2)

    def hop1(k):
        i, j = o_at(k), h_at(k)
        to_q = remote(g_hbm.at[pl.ds(pl.multiple_of(off_h + i * ch, ch), ch)], rq.at[cut(i)], h1_s.at[0, i], h1_r.at[0, i], (w, q))
        to_r = remote(g_hbm.at[pl.ds(pl.multiple_of(off_o + j * ch, ch), ch)], rr.at[cut(j)], h1_s.at[1, j], h1_r.at[1, j], (w, r))
        return to_q, to_r

    def hop2(k):
        i, j = o_at(k), h_at(k)
        to_r = remote(rq.at[cut(i)], part.at[1, cut(i)], h2_s.at[1, i], h2_r.at[1, i], (w, r))
        to_q = remote(rr.at[cut(j)], part.at[0, cut(j)], h2_s.at[0, j], h2_r.at[0, j], (w, q))
        return to_r, to_q

    def start(copies):
        for c in copies:
            c.start()

    start(first_pushes())
    start(hop1(0))
    load("gh", 0, g_hbm.at[pl.ds(off_h, half)], g2.at[0])
    load("go", 1, g_hbm.at[pl.ds(off_o, half)], g2.at[1])
    load("x2h", 2, x_hbm.at[2, pl.ds(off_h, half)], xv.at[2, 0])
    load("x2o", 3, x_hbm.at[2, pl.ds(off_o, half)], xv.at[2, 1])
    c0 = remote(wc_hbm.at[0], far0, c0_s, c0_r, (w, co))
    c0.start()

    def arrived(i):
        wait_for(far.at[i, wy, wx], push_r.at[i])

    arrived(C2_R)
    arrived(A2_Q)
    start(second_pushes())

    @pl.loop(1, NC)
    def _(k):
        start(hop1(k))

    load("a", 4, ws_hbm, av)
    load("c", 5, wc_hbm, cv)
    load("x1h", 6, x_hbm.at[1, pl.ds(off_h, half)], xv.at[1, 0])
    load("x1o", 7, x_hbm.at[1, pl.ds(off_o, half)], xv.at[1, 1])
    load("x0h", 8, x_hbm.at[0, pl.ds(off_h, half)], xv.at[0, 0])
    load("x0o", 9, x_hbm.at[0, pl.ds(off_o, half)], xv.at[0, 1])

    def spread(i):
        own = far.at[i, wy, wx, :, left]
        yield remote(own, own, wy1_s.at[i], wy1_r.at[i], beside_y)
        own = far.at[i, wy, wx, :, right]
        for to in beside_x:
            yield remote(own, own, wx1_s.at[i], wx1_r.at[i], to)

    def spread_on(i):
        wait_for(far.at[i, 0, 0, :, left], wy1_r.at[i])
        pairs = far.at[i, :, wx, :, left]
        for to in beside_x:
            remote(pairs, pairs, wx2_s.at[i], wx2_r.at[i], to).start()
        wait_for(far.at[i, 0, pl.ds(0, WX - 1), :, right], wx1_r.at[i])
        fours = far.at[i, wy, :, :, right]
        remote(fours, fours, wy2_s.at[i], wy2_r.at[i], beside_y).start()

    start(spread(C2_R))
    start(spread(A2_Q))

    def scatter(t):
        for d, v in enumerate(x_peers):
            remote(sb.at[t, :, v, :, left], got_x.at[t, d], sx1_s.at[t], sx1_r.at[t], beside_x[d]).start()
        remote(sb.at[t, oy, :, :, right], got_y.at[t], sy1_s.at[t], sy1_r.at[t], beside_y).start()

    def scatter_on(t):
        wait_for(got_y.at[t], sy1_r.at[t])
        for v in range(WX):
            y = acc[t, rows_of(wy, v), right] + got_y[t, v].astype(jnp.float32)
            sum_y[t, v] = y.astype(jnp.bfloat16)
            own_y[v] = y
        wait_for(got_x.at[t], sx1_r.at[t])

        def sum_left(y):
            total = acc[t, rows_of(y, wx), left]
            for d in range(WX - 1):
                total = total + got_x[t, d, y].astype(jnp.float32)
            return total

        sum_x[t] = sum_left(oy).astype(jnp.bfloat16)
        to_x, to_y = (across_x, across_y) if t == CROSS0 else (beside_x, beside_y)
        for d, v in enumerate(x_peers):
            remote(sum_y.at[t, v], end_x.at[t, d], sx2_s.at[t], sx2_r.at[t], to_x[d]).start()
        own_x[t, :, left] = sum_left(wy)
        own_x[t, :, right] = own_y[wx]
        remote(sum_x.at[t], end_y.at[t], sy2_s.at[t], sy2_r.at[t], to_y).start()

    def own_across():
        return remote(own_x.at[CROSS0], got_own, co_s, co_r, (w, co))

    def total_of(t):
        if t == CROSS0:
            own_across().wait_recv()
        own = got_own if t == CROSS0 else own_x.at[t]
        wait_for(end_x.at[t], sx2_r.at[t])
        total = own[:, right]
        for d in range(WX - 1):
            total = total + end_x[t, d].astype(jnp.float32)
        wait_for(end_y.at[t], sy2_r.at[t])
        first = own[:, left] + end_y[t].astype(jnp.float32)
        return first * scale, total * scale

    def finish(t, out, level):
        a, b = total_of(t)
        out[level, :, left] = a
        out[level, :, right] = b

    def finish_self(t, level):
        finish(t, gsv, level)

    def cross_back(level):
        return remote(res.at[level], gcv.at[level], cr_s.at[level], cr_r.at[level], (w, flip(n, 1 << level)))

    def finish_cross(t, level):
        finish(t, res, level)
        cross_back(level).start()

    def pack(t):
        sb[t] = acc[t].astype(jnp.bfloat16).reshape(sb.shape[1:])

    for name in ("gh", "go", "x2h", "x2o"):
        loads[name].wait()
    for s in range(2):
        d = outer(xv[2, s], g2[s])
        if s == 0:
            acc[SELF2] = d
        else:
            acc[SELF2] += d
    pack(SELF2)

    for i in (C2_P, A2_P, C1_Q):
        arrived(i)
        start(spread(i))
    scatter(SELF2)

    def gathered(i):
        wait_for(far.at[i, :, pl.ds(0, WX - 1), :, left], wx2_r.at[i])
        wait_for(far.at[i, 0, :, :, right], wy2_r.at[i])

    for t in (CROSS2, SELF1, CROSS1, CROSS0, SELF0):
        acc[t] = jnp.zeros((blk, blk), jnp.float32)

    def relay(k):
        to_q, to_r = hop1(k)
        to_r2, to_q2 = hop2(k)
        to_q.wait_recv()
        to_r2.start()
        to_r.wait_recv()
        to_q2.start()

    for k in range(NC // 2):
        relay(k)
    for i in (C2_R, A2_Q, C2_P):
        spread_on(i)
    for k in range(NC // 2, NC - NC // 4):
        relay(k)
    for i in (A2_P, C1_Q):
        spread_on(i)
    scatter_on(SELF2)
    for k in range(NC - NC // 4, NC):
        relay(k)

    for name in ("a", "c", "x1h", "x1o", "x0h", "x0o"):
        loads[name].wait()
    for i in range(5):
        gathered(i)
    c0.wait_recv()

    def foreign(i):
        return far[i].reshape(blk, blk)

    @pl.loop(0, NC)
    def _(k):
        s = cut(k)
        y = trans(rq[s], foreign(A2_Q)) + trans(rr[s], foreign(C2_R))
        g1q[0, s] = y.astype(jnp.bfloat16)

    def level2(side, k):
        s = cut(k)
        g = part[side, s]
        acc[CROSS2] += outer(xv[2, side, s], g)
        y = trans(g2[side, s], av[2]) + trans(g, foreign(C2_P))
        y = y.astype(jnp.bfloat16)
        g1z[side, s] = y
        acc[SELF1] += outer(xv[1, side, s], y)

    def level0_send(side, k):
        s = cut(k)
        return remote(g0z.at[side, s], g0o.at[side, s], l0_s.at[side, k], l0_r.at[side, k], (w, co))

    def level1(side, k):
        s = cut(k)
        y = trans(g1z[side, s], av[1]) + trans(g1q[side, s], foreign(C1_Q))
        g0z[side, s] = y.astype(jnp.bfloat16)

    def pair(k):
        return pl.ds(pl.multiple_of(2 * k * ch, 2 * ch), 2 * ch)

    def add(t, level, side, s, g):
        acc[t] += outer(xv[level, side, s], g[side, s])

    def last(side):
        @pl.loop(0, NC // 2)
        def _(k):
            s = pair(k)
            y = trans(g0z[side, s], av[0]) + trans(g0o[side, s], far0[...])
            outv[side, s] = y.astype(jnp.bfloat16)

    def level1_sends(k):
        to_q = remote(g1z.at[1, cut(2 * k)], g1q.at[1, cut(2 * k)], l1_s.at[0, k], l1_r.at[0, k], (w, q))
        to_r = remote(help1.at[cut(k)], g1q.at[1, cut(2 * k + 1)], l1_s.at[1, k], l1_r.at[1, k], (w, r))
        return to_q, to_r

    @pl.loop(0, NC)
    def _(k):
        i, j = o_at(k), h_at(k)
        to_r2, to_q2 = hop2(k)
        to_q2.wait_recv()

        @pl.when(k < NC // 2)
        def _():
            s = cut(j)
            y = trans(part[0, s], foreign(A2_P)) + trans(g2[0, s], cv[2])
            help1[cut(k)] = y.astype(jnp.bfloat16)

        to_r2.wait_recv()
        level2(1, i)

        @pl.when(k < NC // 2)
        def _():
            start(level1_sends(k))

        level2(0, j)

        @pl.when(k == NC - 1)
        def _():
            pack(CROSS2)
            pack(SELF1)

        level1(0, j)

        @pl.when(k == NC - 1)
        def _():
            scatter(CROSS2)
            scatter(SELF1)

        level0_send(0, j).start()

    @pl.loop(0, NC // 2)
    def _(k):
        s = pair(k)
        add(CROSS1, 1, 0, s, g1q)
        add(SELF0, 0, 0, s, g0z)
        level0_send(0, 2 * k).wait_recv()
        level0_send(0, 2 * k + 1).wait_recv()
        add(CROSS0, 0, 0, s, g0o)

    @pl.loop(0, NC // 2)
    def _(k):
        s = pair(k)
        to_q, to_r = level1_sends(k)
        ends = k == NC // 2 - 1

        @pl.when(ends)
        def _():
            scatter_on(CROSS2)
            scatter_on(SELF1)
            finish_self(SELF2, 2)

        to_q.wait_recv()
        to_r.wait_recv()
        add(CROSS1, 1, 1, s, g1q)

        @pl.when(ends)
        def _():
            pack(CROSS1)

        level1(1, 2 * k)

        @pl.when(ends)
        def _():
            scatter(CROSS1)

        level1(1, 2 * k + 1)
        level0_send(1, 2 * k).start()
        level0_send(1, 2 * k + 1).start()
        add(SELF0, 0, 1, s, g0z)

        @pl.when(ends)
        def _():
            pack(SELF0)

        level0_send(1, 2 * k).wait_recv()

        @pl.when(ends)
        def _():
            scatter(SELF0)

        level0_send(1, 2 * k + 1).wait_recv()
        add(CROSS0, 0, 1, s, g0o)

        @pl.when(ends)
        def _():
            pack(CROSS0)

    finish_cross(CROSS2, 2)
    scatter_on(CROSS1)
    scatter(CROSS0)
    last(0)
    finish_self(SELF1, 1)
    scatter_on(SELF0)
    finish_cross(CROSS1, 1)
    last(1)
    scatter_on(CROSS0)
    own_across().start()
    finish_self(SELF0, 0)
    finish(CROSS0, gcv, 0)
    own_across().wait_send()
    for level in (1, 2):
        cross_back(level).wait()

    for c in first_pushes() + second_pushes():
        c.wait_send()
    c0.wait_send()

    @pl.loop(0, NC)
    def _(k):
        for c in hop1(k) + hop2(k) + (level0_send(0, k), level0_send(1, k)):
            c.wait_send()

    @pl.loop(0, NC // 2)
    def _(k):
        for c in level1_sends(k):
            c.wait_send()

    for i in range(5):
        wait_for(far.at[i, 0, 0, :, left], wy1_s.at[i])
        wait_for(far.at[i, 0, pl.ds(0, WX - 1), :, right], wx1_s.at[i])
        wait_for(far.at[i, :, pl.ds(0, WX - 1), :, left], wx2_s.at[i])
        wait_for(far.at[i, 0, :, :, right], wy2_s.at[i])
    for t in range(6):
        wait_for(got_x.at[t], sx1_s.at[t])
        wait_for(got_y.at[t], sy1_s.at[t])
        wait_for(end_y.at[t], sy2_s.at[t])
        wait_for(end_x.at[t], sx2_s.at[t])


def write_out(outv, gsv, gcv, out_hbm, gs_hbm, gc_hbm, sem):
    n = lax.axis_index("narrow")
    half = outv.shape[1]
    h = lax.rem(lax.div(n, 4), 2)
    copies = []
    for i, (src, dst) in enumerate((
        (outv.at[0], out_hbm.at[pl.ds(pl.multiple_of(h * half, half), half)]),
        (outv.at[1], out_hbm.at[pl.ds(pl.multiple_of((1 - h) * half, half), half)]),
        (gsv, gs_hbm),
        (gcv, gc_hbm),
    )):
        c = pltpu.make_async_copy(src, dst, sem.at[i])
        c.start()
        copies.append(c)
    for c in copies:
        c.wait()


def local(saved_inputs, cotangent, w_self, w_cross):
    wide = lax.axis_size("wide")
    tokens, blk = cotangent.shape
    scale = 1.0 / math.sqrt(tokens * wide)
    half, rows, cols = tokens // 2, blk // wide, blk // 2
    bf, f32 = jnp.bfloat16, jnp.float32
    dma = pltpu.SemaphoreType.DMA
    both = pltpu.VMEM((2, half, blk), bf)
    square3 = pltpu.VMEM((3, blk, blk), bf)

    def body(*refs):
        kernel(wide, scale, *refs)

    vmem, anywhere = pl.BlockSpec(memory_space=pltpu.VMEM), pl.BlockSpec(memory_space=pl.ANY)
    kept = pl.pallas_call(
        body,
        out_shape=(
            pltpu.VMEM((2, half, blk), bf),
            pltpu.VMEM((LEVELS, rows, blk), f32),
            pltpu.VMEM((LEVELS, rows, blk), f32),
        ),
        in_specs=[anywhere] * 4,
        out_specs=[vmem] * 3,
        scratch_shapes=[
            pltpu.VMEM((3, 2, half, blk), bf),
            both,
            square3, square3,
            pltpu.VMEM((5, 2, WX, rows, blk), bf),
            pltpu.VMEM((blk, blk), bf),
            pltpu.VMEM((half, blk), bf), pltpu.VMEM((half, blk), bf),
            both, both, both,
            pltpu.VMEM((half // 2, blk), bf),
            both, both,
            pltpu.VMEM((6, blk, blk), f32),
            pltpu.VMEM((6, 2, WX, rows, blk), bf),
            pltpu.VMEM((rows, blk), f32),
            pltpu.VMEM((6, WX - 1, 2, rows, cols), bf),
            pltpu.VMEM((6, WX, rows, cols), bf),
            pltpu.VMEM((6, rows, cols), bf),
            pltpu.VMEM((6, WX, rows, cols), bf),
            pltpu.VMEM((6, rows, blk), f32),
            pltpu.VMEM((WX, rows, cols), f32),
            pltpu.VMEM((6, rows, cols), bf),
            pltpu.VMEM((6, WX - 1, rows, cols), bf),
            pltpu.VMEM((3, rows, blk), f32),
            dma((10,)),
            dma((5,)), dma((5,)),
            *[dma((5,))] * 8,
            dma(()), dma(()),
            dma((2, NC)), dma((2, NC)), dma((2, NC)), dma((2, NC)),
            dma((2, NC // 2)), dma((2, NC // 2)),
            dma((2, NC)), dma((2, NC)),
            *[dma((6,))] * 8,
            dma((3,)), dma((3,)),
            dma(()), dma(()),
        ],
        compiler_params=pltpu.CompilerParams(
            collective_id=0, has_side_effects=True, vmem_limit_bytes=60 << 20
        ),
        name="butterfly_backward",
    )(saved_inputs, cotangent, w_self, w_cross)
    return pl.pallas_call(
        write_out,
        out_shape=(
            jax.ShapeDtypeStruct((tokens, blk), bf),
            jax.ShapeDtypeStruct((LEVELS, rows, blk), f32),
            jax.ShapeDtypeStruct((LEVELS, rows, blk), f32),
        ),
        in_specs=[vmem] * 3,
        out_specs=[anywhere] * 3,
        scratch_shapes=[dma((4,))],
        compiler_params=pltpu.CompilerParams(vmem_limit_bytes=8 << 20),
        name="write_out",
    )(*kept)


def solution(mesh):
    in_specs = (
        P(None, "wide", "narrow"),
        P("wide", "narrow"),
        P(None, "narrow", None),
        P(None, "narrow", None),
    )
    out_specs = (
        P("wide", "narrow"),
        P(None, ("narrow", "wide"), None),
        P(None, ("narrow", "wide"), None),
    )
    return jax.shard_map(local, mesh=mesh, in_specs=in_specs, out_specs=out_specs, check_vma=False)
```

```python
import math

import jax
import jax.numpy as jnp
from jax import lax
from jax.experimental import pallas as pl
from jax.experimental.pallas import tpu as pltpu
from jax.sharding import PartitionSpec as P

LEVELS = 3
NC = 4
WX = 4
MESH = pl.DeviceIdType.MESH

C2_P, A2_Q, C2_R, A2_P, C1_Q = range(5)
SELF2, CROSS2, SELF1, CROSS1, CROSS0, SELF0 = range(6)


def flip(n, bit):
    return n + bit - 2 * bit * lax.rem(lax.div(n, bit), 2)


def outer(left, right):
    return lax.dot_general(left, right, (((0,), (0,)), ((), ())), preferred_element_type=jnp.float32)


def trans(left, right):
    return lax.dot_general(left, right, (((1,), (1,)), ((), ())), preferred_element_type=jnp.float32)


def remote(src, dst, send, recv, to):
    return pltpu.make_async_remote_copy(
        src_ref=src, dst_ref=dst, send_sem=send, recv_sem=recv, device_id=to, device_id_type=MESH
    )


def wait_for(ref, sem):
    pltpu.make_async_copy(ref, ref, sem).wait()


def kernel(
    wide, scale,
    x_hbm, g_hbm, ws_hbm, wc_hbm,
    outv, gsv, gcv,
    xv, g2, av, cv, far, far0, rq, rr, part, g1z, g1q, help1, help2, g0z, g0o,
    acc, sb, got_own, got_x, got_y, sum_x, sum_y, own_x, own_y, end_y, end_x, res,
    ld, push_s, push_r, wy1_s, wy1_r, wx1_s, wx1_r, wx2_s, wx2_r, wy2_s, wy2_r, c0_s, c0_r, h1_s, h1_r, h2_s, h2_r,
    l1_s, l1_r, l0_s, l0_r, sx1_s, sx1_r, sy1_s, sy1_r, sy2_s, sy2_r, sx2_s, sx2_r, cr_s, cr_r, co_s, co_r, ex_s, ex_r,
):
    w = lax.axis_index("wide")
    n = lax.axis_index("narrow")
    wx, wy = lax.rem(w, WX), lax.div(w, WX)
    oy = 1 - wy
    x_peers = [lax.rem(wx + dx, WX) for dx in (1, 3, 2)]
    q, r, p, co = flip(n, 2), flip(flip(n, 2), 4), flip(n, 4), flip(n, 1)
    half = g2.shape[1]
    ch = half // NC
    blk = g2.shape[2]
    rows = blk // wide
    cols = blk // 2
    left, right = pl.ds(0, cols), pl.ds(cols, cols)
    beside_x = [(wy * WX + v, n) for v in x_peers]
    beside_y = (oy * WX + wx, n)
    across_x = [(v, co) for v, _ in beside_x]
    across_y = (oy * WX + wx, co)
    h = lax.rem(lax.div(n, 4), 2)
    extra = ch // 8
    extra_rows = pl.ds(3 * ch - extra, extra)
    off_h = pl.multiple_of(h * half, half)
    off_o = pl.multiple_of((1 - h) * half, half)
    mine = pl.ds(pl.multiple_of(w * rows, rows), rows)

    def rows_of(y, x, many=1):
        return pl.ds(pl.multiple_of((y * WX + x) * rows, rows), many * rows)

    def cut(k):
        return pl.ds(pl.multiple_of(k * ch, ch), ch)

    loads = {}

    def load(name, i, src, dst):
        c = pltpu.make_async_copy(src, dst, ld.at[i])
        c.start()
        loads[name] = c

    barrier = pltpu.get_barrier_semaphore()
    for other in [(w, q), (w, r), (w, p), (w, co), beside_y, across_y] + beside_x + across_x:
        pl.semaphore_signal(barrier, inc=1, device_id=other, device_id_type=MESH)
    pl.semaphore_wait(barrier, 6 + 2 * len(beside_x))

    def push(i, src, to):
        return remote(src, far.at[i, wy, wx], push_s.at[i], push_r.at[i], (w, to))

    def first_pushes():
        return (
            push(C2_R, wc_hbm.at[2, mine], r),
            push(A2_Q, ws_hbm.at[2, mine], q),
            push(C1_Q, wc_hbm.at[1, mine], q),
        )

    def second_pushes():
        return push(C2_P, far.at[C2_R, wy, wx], q), push(A2_P, far.at[A2_Q, wy, wx], r)

    def h_at(k):
        return lax.rem(2 * k, NC) + 1 - lax.div(k, NC // 2)

    def o_at(k):
        return lax.rem(2 * k, NC) + lax.div(k, NC // 2)

    def hop1(k):
        i, j = o_at(k), h_at(k)
        to_q = remote(g_hbm.at[pl.ds(pl.multiple_of(off_h + i * ch, ch), ch)], rq.at[cut(i)], h1_s.at[0, i], h1_r.at[0, i], (w, q))
        to_r = remote(g_hbm.at[pl.ds(pl.multiple_of(off_o + j * ch, ch), ch)], rr.at[cut(j)], h1_s.at[1, j], h1_r.at[1, j], (w, r))
        return to_q, to_r

    def hop2(k):
        i, j = o_at(k), h_at(k)
        to_r = remote(rq.at[cut(i)], part.at[1, cut(i)], h2_s.at[1, i], h2_r.at[1, i], (w, r))
        to_q = remote(rr.at[cut(j)], part.at[0, cut(j)], h2_s.at[0, j], h2_r.at[0, j], (w, q))
        return to_r, to_q

    def start(copies):
        for c in copies:
            c.start()

    start(first_pushes())
    start(hop1(0))
    load("gh", 0, g_hbm.at[pl.ds(off_h, half)], g2.at[0])
    load("go", 1, g_hbm.at[pl.ds(off_o, half)], g2.at[1])
    load("x2h", 2, x_hbm.at[2, pl.ds(off_h, half)], xv.at[2, 0])
    load("x2o", 3, x_hbm.at[2, pl.ds(off_o, half)], xv.at[2, 1])
    c0 = remote(wc_hbm.at[0], far0, c0_s, c0_r, (w, co))
    c0.start()

    def arrived(i):
        wait_for(far.at[i, wy, wx], push_r.at[i])

    arrived(C2_R)
    arrived(A2_Q)
    start(second_pushes())

    @pl.loop(1, NC)
    def _(k):
        start(hop1(k))

    load("a", 4, ws_hbm, av)
    load("c", 5, wc_hbm, cv)
    load("x1h", 6, x_hbm.at[1, pl.ds(off_h, half)], xv.at[1, 0])
    load("x1o", 7, x_hbm.at[1, pl.ds(off_o, half)], xv.at[1, 1])
    load("x0h", 8, x_hbm.at[0, pl.ds(off_h, half)], xv.at[0, 0])
    load("x0o", 9, x_hbm.at[0, pl.ds(off_o, half)], xv.at[0, 1])

    def spread(i):
        own = far.at[i, wy, wx, :, left]
        yield remote(own, own, wy1_s.at[i], wy1_r.at[i], beside_y)
        own = far.at[i, wy, wx, :, right]
        for to in beside_x:
            yield remote(own, own, wx1_s.at[i], wx1_r.at[i], to)

    def spread_on(i):
        wait_for(far.at[i, 0, 0, :, left], wy1_r.at[i])
        pairs = far.at[i, :, wx, :, left]
        for to in beside_x:
            remote(pairs, pairs, wx2_s.at[i], wx2_r.at[i], to).start()
        wait_for(far.at[i, 0, pl.ds(0, WX - 1), :, right], wx1_r.at[i])
        fours = far.at[i, wy, :, :, right]
        remote(fours, fours, wy2_s.at[i], wy2_r.at[i], beside_y).start()

    start(spread(C2_R))
    start(spread(A2_Q))

    def scatter(t):
        for d, v in enumerate(x_peers):
            remote(sb.at[t, :, v, :, left], got_x.at[t, d], sx1_s.at[t], sx1_r.at[t], beside_x[d]).start()
        remote(sb.at[t, oy, :, :, right], got_y.at[t], sy1_s.at[t], sy1_r.at[t], beside_y).start()

    def scatter_on(t):
        wait_for(got_y.at[t], sy1_r.at[t])
        for v in range(WX):
            y = acc[t, rows_of(wy, v), right] + got_y[t, v].astype(jnp.float32)
            sum_y[t, v] = y.astype(jnp.bfloat16)
            own_y[v] = y
        wait_for(got_x.at[t], sx1_r.at[t])

        def sum_left(y):
            total = acc[t, rows_of(y, wx), left]
            for d in range(WX - 1):
                total = total + got_x[t, d, y].astype(jnp.float32)
            return total

        sum_x[t] = sum_left(oy).astype(jnp.bfloat16)
        to_x, to_y = (across_x, across_y) if t == CROSS0 else (beside_x, beside_y)
        for d, v in enumerate(x_peers):
            remote(sum_y.at[t, v], end_x.at[t, d], sx2_s.at[t], sx2_r.at[t], to_x[d]).start()
        own_x[t, :, left] = sum_left(wy)
        own_x[t, :, right] = own_y[wx]
        remote(sum_x.at[t], end_y.at[t], sy2_s.at[t], sy2_r.at[t], to_y).start()

    def own_across():
        return remote(own_x.at[CROSS0], got_own, co_s, co_r, (w, co))

    def total_of(t):
        if t == CROSS0:
            own_across().wait_recv()
        own = got_own if t == CROSS0 else own_x.at[t]
        wait_for(end_x.at[t], sx2_r.at[t])
        total = own[:, right]
        for d in range(WX - 1):
            total = total + end_x[t, d].astype(jnp.float32)
        wait_for(end_y.at[t], sy2_r.at[t])
        first = own[:, left] + end_y[t].astype(jnp.float32)
        return first * scale, total * scale

    def finish(t, out, level):
        a, b = total_of(t)
        out[level, :, left] = a
        out[level, :, right] = b

    def finish_self(t, level):
        finish(t, gsv, level)

    def cross_back(level):
        return remote(res.at[level], gcv.at[level], cr_s.at[level], cr_r.at[level], (w, flip(n, 1 << level)))

    def finish_cross(t, level):
        finish(t, res, level)
        cross_back(level).start()

    def pack(t):
        sb[t] = acc[t].astype(jnp.bfloat16).reshape(sb.shape[1:])

    for name in ("gh", "go", "x2h", "x2o"):
        loads[name].wait()
    for s in range(2):
        d = outer(xv[2, s], g2[s])
        if s == 0:
            acc[SELF2] = d
        else:
            acc[SELF2] += d
    pack(SELF2)

    for i in (C2_P, A2_P, C1_Q):
        arrived(i)
        start(spread(i))
    scatter(SELF2)

    def gathered(i):
        wait_for(far.at[i, :, pl.ds(0, WX - 1), :, left], wx2_r.at[i])
        wait_for(far.at[i, 0, :, :, right], wy2_r.at[i])

    for t in (CROSS2, SELF1, CROSS1, CROSS0, SELF0):
        acc[t] = jnp.zeros((blk, blk), jnp.float32)

    def relay(k):
        to_q, to_r = hop1(k)
        to_r2, to_q2 = hop2(k)
        to_q.wait_recv()
        to_r2.start()
        to_r.wait_recv()
        to_q2.start()

    for k in range(NC // 2):
        relay(k)
    for i in (C2_R, A2_Q, C2_P):
        spread_on(i)
    for k in range(NC // 2, NC - NC // 4):
        relay(k)
    for i in (A2_P, C1_Q):
        spread_on(i)
    scatter_on(SELF2)
    for k in range(NC - NC // 4, NC):
        relay(k)

    for name in ("a", "c", "x1h", "x1o", "x0h", "x0o"):
        loads[name].wait()
    for i in range(5):
        gathered(i)
    c0.wait_recv()

    def foreign(i):
        return far[i].reshape(blk, blk)

    @pl.loop(0, NC)
    def _(k):
        s = cut(k)
        y = trans(rq[s], foreign(A2_Q)) + trans(rr[s], foreign(C2_R))
        y = y.astype(jnp.bfloat16)
        g1q[0, s] = y
        acc[CROSS1] += outer(xv[1, 0, s], y)

    def level2(side, k):
        s = cut(k)
        g = part[side, s]
        acc[CROSS2] += outer(xv[2, side, s], g)
        y = trans(g2[side, s], av[2]) + trans(g, foreign(C2_P))
        y = y.astype(jnp.bfloat16)
        g1z[side, s] = y
        acc[SELF1] += outer(xv[1, side, s], y)

    def level0_send(side, k):
        s = cut(k)
        return remote(g0z.at[side, s], g0o.at[side, s], l0_s.at[side, k], l0_r.at[side, k], (w, co))

    def level1(side, k):
        s = cut(k)
        y = trans(g1z[side, s], av[1]) + trans(g1q[side, s], foreign(C1_Q))
        g0z[side, s] = y.astype(jnp.bfloat16)

    def pair(k):
        return pl.ds(pl.multiple_of(2 * k * ch, 2 * ch), 2 * ch)

    def add(t, level, side, s, g):
        acc[t] += outer(xv[level, side, s], g[side, s])

    def level0_of(j):
        s = cut(j)
        add(SELF0, 0, 0, s, g0z)
        level0_send(0, j).wait_recv()
        add(CROSS0, 0, 0, s, g0o)

    def last(side):
        @pl.loop(0, NC // 2)
        def _(k):
            s = pair(k)
            y = trans(g0z[side, s], av[0]) + trans(g0o[side, s], far0[...])
            outv[side, s] = y.astype(jnp.bfloat16)

    def extra_send():
        return remote(help2, g1q.at[1, extra_rows], ex_s, ex_r, (w, r))

    def level1_sends(k):
        n_q = ch if k == 0 else ch - extra
        s = pl.ds(2 * k * ch, n_q)
        to_q = remote(g1z.at[1, s], g1q.at[1, s], l1_s.at[0, k], l1_r.at[0, k], (w, q))
        to_r = remote(help1.at[cut(k)], g1q.at[1, cut(2 * k + 1)], l1_s.at[1, k], l1_r.at[1, k], (w, r))
        return to_q, to_r

    @pl.loop(0, NC)
    def _(k):
        i, j = o_at(k), h_at(k)

        @pl.when(k > 0)
        def _():
            level0_of(h_at(k - 1))

        to_r2, to_q2 = hop2(k)
        to_q2.wait_recv()

        @pl.when(k < NC // 2)
        def _():
            s = cut(j)
            y = trans(part[0, s], foreign(A2_P)) + trans(g2[0, s], cv[2])
            help1[cut(k)] = y.astype(jnp.bfloat16)

        @pl.when(k == NC - 1)
        def _():
            y = trans(part[0, extra_rows], foreign(A2_P)) + trans(g2[0, extra_rows], cv[2])
            help2[...] = y.astype(jnp.bfloat16)

        to_r2.wait_recv()
        level2(1, i)

        for kk in range(NC // 2):
            @pl.when(k == kk)
            def _():
                start(level1_sends(kk))

        @pl.when(k == NC - 1)
        def _():
            extra_send().start()

        level2(0, j)

        @pl.when(k == NC - 1)
        def _():
            pack(CROSS2)
            pack(SELF1)

        level1(0, j)

        @pl.when(k == NC - 1)
        def _():
            scatter(CROSS2)
            scatter(SELF1)

        level0_send(0, j).start()

    level0_of(h_at(NC - 1))

    for k in range(NC // 2):
        s = pair(k)
        to_q, to_r = level1_sends(k)
        ends = k == NC // 2 - 1

        if ends:
            scatter_on(CROSS2)
            scatter_on(SELF1)
            finish_self(SELF2, 2)

        to_q.wait_recv()
        to_r.wait_recv()
        if ends:
            extra_send().wait_recv()
        add(CROSS1, 1, 1, s, g1q)

        if ends:
            pack(CROSS1)

        level1(1, 2 * k)

        if ends:
            scatter(CROSS1)

        level1(1, 2 * k + 1)
        level0_send(1, 2 * k).start()
        level0_send(1, 2 * k + 1).start()
        add(SELF0, 0, 1, s, g0z)

        if ends:
            pack(SELF0)

        level0_send(1, 2 * k).wait_recv()

        if ends:
            scatter(SELF0)

        level0_send(1, 2 * k + 1).wait_recv()
        add(CROSS0, 0, 1, s, g0o)

        if ends:
            pack(CROSS0)

    finish_cross(CROSS2, 2)
    scatter_on(CROSS1)
    scatter(CROSS0)
    last(0)
    finish_self(SELF1, 1)
    scatter_on(SELF0)
    finish_cross(CROSS1, 1)
    last(1)
    scatter_on(CROSS0)
    own_across().start()
    finish_self(SELF0, 0)
    finish(CROSS0, gcv, 0)
    own_across().wait_send()
    for level in (1, 2):
        cross_back(level).wait()

    for c in first_pushes() + second_pushes():
        c.wait_send()
    c0.wait_send()

    @pl.loop(0, NC)
    def _(k):
        for c in hop1(k) + hop2(k) + (level0_send(0, k), level0_send(1, k)):
            c.wait_send()

    for k in range(NC // 2):
        for c in level1_sends(k):
            c.wait_send()
    extra_send().wait_send()

    for i in range(5):
        wait_for(far.at[i, 0, 0, :, left], wy1_s.at[i])
        wait_for(far.at[i, 0, pl.ds(0, WX - 1), :, right], wx1_s.at[i])
        wait_for(far.at[i, :, pl.ds(0, WX - 1), :, left], wx2_s.at[i])
        wait_for(far.at[i, 0, :, :, right], wy2_s.at[i])
    for t in range(6):
        wait_for(got_x.at[t], sx1_s.at[t])
        wait_for(got_y.at[t], sy1_s.at[t])
        wait_for(end_y.at[t], sy2_s.at[t])
        wait_for(end_x.at[t], sx2_s.at[t])


def write_out(outv, gsv, gcv, out_hbm, gs_hbm, gc_hbm, sem):
    n = lax.axis_index("narrow")
    half = outv.shape[1]
    h = lax.rem(lax.div(n, 4), 2)
    copies = []
    for i, (src, dst) in enumerate((
        (outv.at[0], out_hbm.at[pl.ds(pl.multiple_of(h * half, half), half)]),
        (outv.at[1], out_hbm.at[pl.ds(pl.multiple_of((1 - h) * half, half), half)]),
        (gsv, gs_hbm),
        (gcv, gc_hbm),
    )):
        c = pltpu.make_async_copy(src, dst, sem.at[i])
        c.start()
        copies.append(c)
    for c in copies:
        c.wait()


def local(saved_inputs, cotangent, w_self, w_cross):
    wide = lax.axis_size("wide")
    tokens, blk = cotangent.shape
    scale = 1.0 / math.sqrt(tokens * wide)
    half, rows, cols = tokens // 2, blk // wide, blk // 2
    bf, f32 = jnp.bfloat16, jnp.float32
    dma = pltpu.SemaphoreType.DMA
    both = pltpu.VMEM((2, half, blk), bf)
    square3 = pltpu.VMEM((3, blk, blk), bf)

    def body(*refs):
        kernel(wide, scale, *refs)

    vmem, anywhere = pl.BlockSpec(memory_space=pltpu.VMEM), pl.BlockSpec(memory_space=pl.ANY)
    kept = pl.pallas_call(
        body,
        out_shape=(
            pltpu.VMEM((2, half, blk), bf),
            pltpu.VMEM((LEVELS, rows, blk), f32),
            pltpu.VMEM((LEVELS, rows, blk), f32),
        ),
        in_specs=[anywhere] * 4,
        out_specs=[vmem] * 3,
        scratch_shapes=[
            pltpu.VMEM((3, 2, half, blk), bf),
            both,
            square3, square3,
            pltpu.VMEM((5, 2, WX, rows, blk), bf),
            pltpu.VMEM((blk, blk), bf),
            pltpu.VMEM((half, blk), bf), pltpu.VMEM((half, blk), bf),
            both, both, both,
            pltpu.VMEM((half // 2, blk), bf),
            pltpu.VMEM((half // NC // 8, blk), bf),
            both, both,
            pltpu.VMEM((6, blk, blk), f32),
            pltpu.VMEM((6, 2, WX, rows, blk), bf),
            pltpu.VMEM((rows, blk), f32),
            pltpu.VMEM((6, WX - 1, 2, rows, cols), bf),
            pltpu.VMEM((6, WX, rows, cols), bf),
            pltpu.VMEM((6, rows, cols), bf),
            pltpu.VMEM((6, WX, rows, cols), bf),
            pltpu.VMEM((6, rows, blk), f32),
            pltpu.VMEM((WX, rows, cols), f32),
            pltpu.VMEM((6, rows, cols), bf),
            pltpu.VMEM((6, WX - 1, rows, cols), bf),
            pltpu.VMEM((3, rows, blk), f32),
            dma((10,)),
            dma((5,)), dma((5,)),
            *[dma((5,))] * 8,
            dma(()), dma(()),
            dma((2, NC)), dma((2, NC)), dma((2, NC)), dma((2, NC)),
            dma((2, NC // 2)), dma((2, NC // 2)),
            dma((2, NC)), dma((2, NC)),
            *[dma((6,))] * 8,
            dma((3,)), dma((3,)),
            dma(()), dma(()),
            dma(()), dma(()),
        ],
        compiler_params=pltpu.CompilerParams(
            collective_id=0, has_side_effects=True, vmem_limit_bytes=60 << 20
        ),
        name="butterfly_backward",
    )(saved_inputs, cotangent, w_self, w_cross)
    return pl.pallas_call(
        write_out,
        out_shape=(
            jax.ShapeDtypeStruct((tokens, blk), bf),
            jax.ShapeDtypeStruct((LEVELS, rows, blk), f32),
            jax.ShapeDtypeStruct((LEVELS, rows, blk), f32),
        ),
        in_specs=[vmem] * 3,
        out_specs=[anywhere] * 3,
        scratch_shapes=[dma((4,))],
        compiler_params=pltpu.CompilerParams(vmem_limit_bytes=8 << 20),
        name="write_out",
    )(*kept)


def solution(mesh):
    in_specs = (
        P(None, "wide", "narrow"),
        P("wide", "narrow"),
        P(None, "narrow", None),
        P(None, "narrow", None),
    )
    out_specs = (
        P("wide", "narrow"),
        P(None, ("narrow", "wide"), None),
        P(None, ("narrow", "wide"), None),
    )
    return jax.shard_map(local, mesh=mesh, in_specs=in_specs, out_specs=out_specs, check_vma=False)
```

```python
import math

import jax
import jax.numpy as jnp
from jax import lax
from jax.experimental import pallas as pl
from jax.experimental.pallas import tpu as pltpu
from jax.sharding import PartitionSpec as P

LEVELS = 3
NC = 4
WX = 4
MESH = pl.DeviceIdType.MESH

C2_P, A2_Q, C2_R, A2_P, C1_Q = range(5)
SELF2, CROSS2, SELF1, CROSS1, CROSS0, SELF0 = range(6)


def flip(n, bit):
    return n + bit - 2 * bit * lax.rem(lax.div(n, bit), 2)


def outer(left, right):
    return lax.dot_general(left, right, (((0,), (0,)), ((), ())), preferred_element_type=jnp.float32)


def trans(left, right):
    return lax.dot_general(left, right, (((1,), (1,)), ((), ())), preferred_element_type=jnp.float32)


def remote(src, dst, send, recv, to):
    return pltpu.make_async_remote_copy(
        src_ref=src, dst_ref=dst, send_sem=send, recv_sem=recv, device_id=to, device_id_type=MESH
    )


def wait_for(ref, sem):
    pltpu.make_async_copy(ref, ref, sem).wait()


def kernel(
    wide, scale,
    x_hbm, g_hbm, ws_hbm, wc_hbm,
    outv, gsv, gcv,
    xv, g2, av, cv, far, far0, rq, rr, part, g1z, g1q, help1, help2, g0z, g0o,
    acc, sb, got_own, got_x, got_y, sum_x, sum_y, own_x, own_y, end_y, end_x, res,
    ld, push_s, push_r, wy1_s, wy1_r, wx1_s, wx1_r, wx2_s, wx2_r, wy2_s, wy2_r, c0_s, c0_r, h1_s, h1_r, h2_s, h2_r,
    l1_s, l1_r, l0_s, l0_r, sx1_s, sx1_r, sy1_s, sy1_r, sy2_s, sy2_r, sx2_s, sx2_r, cr_s, cr_r, co_s, co_r, ex_s, ex_r,
):
    w = lax.axis_index("wide")
    n = lax.axis_index("narrow")
    wx, wy = lax.rem(w, WX), lax.div(w, WX)
    oy = 1 - wy
    x_peers = [lax.rem(wx + dx, WX) for dx in (2, 1, 3)]
    q, r, p, co = flip(n, 2), flip(flip(n, 2), 4), flip(n, 4), flip(n, 1)
    half = g2.shape[1]
    ch = half // NC
    blk = g2.shape[2]
    rows = blk // wide
    cols = blk // 2
    left, right = pl.ds(0, cols), pl.ds(cols, cols)
    beside_x = [(wy * WX + v, n) for v in x_peers]
    beside_y = (oy * WX + wx, n)
    across_x = [(v, co) for v, _ in beside_x]
    across_y = (oy * WX + wx, co)
    h = lax.rem(lax.div(n, 4), 2)
    extra = ch // 8
    extra_rows = pl.ds(3 * ch - extra, extra)
    off_h = pl.multiple_of(h * half, half)
    off_o = pl.multiple_of((1 - h) * half, half)
    mine = pl.ds(pl.multiple_of(w * rows, rows), rows)

    def rows_of(y, x, many=1):
        return pl.ds(pl.multiple_of((y * WX + x) * rows, rows), many * rows)

    def cut(k):
        return pl.ds(pl.multiple_of(k * ch, ch), ch)

    loads = {}

    def load(name, i, src, dst):
        c = pltpu.make_async_copy(src, dst, ld.at[i])
        c.start()
        loads[name] = c

    barrier = pltpu.get_barrier_semaphore()
    for other in [(w, q), (w, r), (w, p), (w, co), beside_y, across_y] + beside_x + across_x:
        pl.semaphore_signal(barrier, inc=1, device_id=other, device_id_type=MESH)
    pl.semaphore_wait(barrier, 6 + 2 * len(beside_x))

    def push(i, src, to):
        return remote(src, far.at[i, wy, wx], push_s.at[i], push_r.at[i], (w, to))

    def first_pushes():
        return (
            push(C2_R, wc_hbm.at[2, mine], r),
            push(A2_Q, ws_hbm.at[2, mine], q),
            push(C1_Q, wc_hbm.at[1, mine], q),
        )

    def second_pushes():
        return push(C2_P, far.at[C2_R, wy, wx], q), push(A2_P, far.at[A2_Q, wy, wx], r)

    def h_at(k):
        return lax.rem(2 * k, NC) + 1 - lax.div(k, NC // 2)

    def o_at(k):
        return lax.rem(2 * k, NC) + lax.div(k, NC // 2)

    def hop1(k):
        i, j = o_at(k), h_at(k)
        to_q = remote(g_hbm.at[pl.ds(pl.multiple_of(off_h + i * ch, ch), ch)], rq.at[cut(i)], h1_s.at[0, i], h1_r.at[0, i], (w, q))
        to_r = remote(g_hbm.at[pl.ds(pl.multiple_of(off_o + j * ch, ch), ch)], rr.at[cut(j)], h1_s.at[1, j], h1_r.at[1, j], (w, r))
        return to_q, to_r

    def hop2(k):
        i, j = o_at(k), h_at(k)
        to_r = remote(rq.at[cut(i)], part.at[1, cut(i)], h2_s.at[1, i], h2_r.at[1, i], (w, r))
        to_q = remote(rr.at[cut(j)], part.at[0, cut(j)], h2_s.at[0, j], h2_r.at[0, j], (w, q))
        return to_r, to_q

    def start(copies):
        for c in copies:
            c.start()

    start(first_pushes())
    start(hop1(0))
    load("gh", 0, g_hbm.at[pl.ds(off_h, half)], g2.at[0])
    load("go", 1, g_hbm.at[pl.ds(off_o, half)], g2.at[1])
    load("x2h", 2, x_hbm.at[2, pl.ds(off_h, half)], xv.at[2, 0])
    load("x2o", 3, x_hbm.at[2, pl.ds(off_o, half)], xv.at[2, 1])
    c0 = remote(wc_hbm.at[0], far0, c0_s, c0_r, (w, co))
    c0.start()

    def arrived(i):
        wait_for(far.at[i, wy, wx], push_r.at[i])

    arrived(C2_R)
    arrived(A2_Q)
    start(second_pushes())

    @pl.loop(1, NC)
    def _(k):
        start(hop1(k))

    load("a", 4, ws_hbm, av)
    load("c", 5, wc_hbm, cv)
    load("x1h", 6, x_hbm.at[1, pl.ds(off_h, half)], xv.at[1, 0])
    load("x1o", 7, x_hbm.at[1, pl.ds(off_o, half)], xv.at[1, 1])
    load("x0h", 8, x_hbm.at[0, pl.ds(off_h, half)], xv.at[0, 0])
    load("x0o", 9, x_hbm.at[0, pl.ds(off_o, half)], xv.at[0, 1])

    def spread(i):
        own = far.at[i, wy, wx, :, left]
        yield remote(own, own, wy1_s.at[i], wy1_r.at[i], beside_y)
        own = far.at[i, wy, wx, :, right]
        for to in beside_x:
            yield remote(own, own, wx1_s.at[i], wx1_r.at[i], to)

    def spread_on(i):
        wait_for(far.at[i, 0, 0, :, left], wy1_r.at[i])
        pairs = far.at[i, :, wx, :, left]
        for to in beside_x:
            remote(pairs, pairs, wx2_s.at[i], wx2_r.at[i], to).start()
        wait_for(far.at[i, 0, pl.ds(0, WX - 1), :, right], wx1_r.at[i])
        fours = far.at[i, wy, :, :, right]
        remote(fours, fours, wy2_s.at[i], wy2_r.at[i], beside_y).start()

    start(spread(C2_R))
    start(spread(A2_Q))

    def scatter(t):
        remote(sb.at[t, oy, :, :, right], got_y.at[t], sy1_s.at[t], sy1_r.at[t], beside_y).start()
        for d, v in enumerate(x_peers):
            remote(sb.at[t, :, v, :, left], got_x.at[t, d], sx1_s.at[t], sx1_r.at[t], beside_x[d]).start()

    def scatter_on(t):
        wait_for(got_y.at[t], sy1_r.at[t])
        for v in range(WX):
            y = acc[t, rows_of(wy, v), right] + got_y[t, v].astype(jnp.float32)
            sum_y[t, v] = y.astype(jnp.bfloat16)
            own_y[v] = y
        wait_for(got_x.at[t], sx1_r.at[t])

        def sum_left(y):
            total = acc[t, rows_of(y, wx), left]
            for d in range(WX - 1):
                total = total + got_x[t, d, y].astype(jnp.float32)
            return total

        sum_x[t] = sum_left(oy).astype(jnp.bfloat16)
        to_x, to_y = (across_x, across_y) if t == CROSS0 else (beside_x, beside_y)
        for d, v in enumerate(x_peers):
            remote(sum_y.at[t, v], end_x.at[t, d], sx2_s.at[t], sx2_r.at[t], to_x[d]).start()
        own_x[t, :, left] = sum_left(wy)
        own_x[t, :, right] = own_y[wx]
        remote(sum_x.at[t], end_y.at[t], sy2_s.at[t], sy2_r.at[t], to_y).start()

    def own_across():
        return remote(own_x.at[CROSS0], got_own, co_s, co_r, (w, co))

    def total_of(t):
        if t == CROSS0:
            own_across().wait_recv()
        own = got_own if t == CROSS0 else own_x.at[t]
        wait_for(end_x.at[t], sx2_r.at[t])
        total = own[:, right]
        for d in range(WX - 1):
            total = total + end_x[t, d].astype(jnp.float32)
        wait_for(end_y.at[t], sy2_r.at[t])
        first = own[:, left] + end_y[t].astype(jnp.float32)
        return first * scale, total * scale

    def finish(t, out, level):
        a, b = total_of(t)
        out[level, :, left] = a
        out[level, :, right] = b

    def finish_self(t, level):
        finish(t, gsv, level)

    def cross_back(level):
        return remote(res.at[level], gcv.at[level], cr_s.at[level], cr_r.at[level], (w, flip(n, 1 << level)))

    def finish_cross(t, level):
        finish(t, res, level)
        cross_back(level).start()

    def pack(t):
        sb[t] = acc[t].astype(jnp.bfloat16).reshape(sb.shape[1:])

    for name in ("gh", "go", "x2h", "x2o"):
        loads[name].wait()
    for s in range(2):
        d = outer(xv[2, s], g2[s])
        if s == 0:
            acc[SELF2] = d
        else:
            acc[SELF2] += d
    pack(SELF2)

    for i in (C2_P, A2_P, C1_Q):
        arrived(i)
        start(spread(i))
    scatter(SELF2)

    def gathered(i):
        wait_for(far.at[i, :, pl.ds(0, WX - 1), :, left], wx2_r.at[i])
        wait_for(far.at[i, 0, :, :, right], wy2_r.at[i])

    for t in (CROSS2, SELF1, CROSS1, CROSS0, SELF0):
        acc[t] = jnp.zeros((blk, blk), jnp.float32)

    def relay(k):
        to_q, to_r = hop1(k)
        to_r2, to_q2 = hop2(k)
        to_q.wait_recv()
        to_r2.start()
        to_r.wait_recv()
        to_q2.start()

    for k in range(NC // 2):
        relay(k)
    for i in (C2_R, A2_Q, C2_P):
        spread_on(i)
    for k in range(NC // 2, NC - NC // 4):
        relay(k)
    for i in (A2_P, C1_Q):
        spread_on(i)
    scatter_on(SELF2)
    for k in range(NC - NC // 4, NC):
        relay(k)

    for name in ("a", "c", "x1h", "x1o", "x0h", "x0o"):
        loads[name].wait()
    for i in range(5):
        gathered(i)
    c0.wait_recv()

    def foreign(i):
        return far[i].reshape(blk, blk)

    @pl.loop(0, NC)
    def _(k):
        s = cut(k)
        y = trans(rq[s], foreign(A2_Q)) + trans(rr[s], foreign(C2_R))
        y = y.astype(jnp.bfloat16)
        g1q[0, s] = y
        acc[CROSS1] += outer(xv[1, 0, s], y)

    def level2(side, k):
        s = cut(k)
        g = part[side, s]
        acc[CROSS2] += outer(xv[2, side, s], g)
        y = trans(g2[side, s], av[2]) + trans(g, foreign(C2_P))
        y = y.astype(jnp.bfloat16)
        g1z[side, s] = y
        acc[SELF1] += outer(xv[1, side, s], y)

    def level0_send(side, k):
        s = cut(k)
        return remote(g0z.at[side, s], g0o.at[side, s], l0_s.at[side, k], l0_r.at[side, k], (w, co))

    def level1(side, k):
        s = cut(k)
        y = trans(g1z[side, s], av[1]) + trans(g1q[side, s], foreign(C1_Q))
        g0z[side, s] = y.astype(jnp.bfloat16)

    def pair(k):
        return pl.ds(pl.multiple_of(2 * k * ch, 2 * ch), 2 * ch)

    def add(t, level, side, s, g):
        acc[t] += outer(xv[level, side, s], g[side, s])

    def level0_of(j):
        s = cut(j)
        add(SELF0, 0, 0, s, g0z)
        level0_send(0, j).wait_recv()
        add(CROSS0, 0, 0, s, g0o)

    def last(side):
        @pl.loop(0, NC // 2)
        def _(k):
            s = pair(k)
            y = trans(g0z[side, s], av[0]) + trans(g0o[side, s], far0[...])
            outv[side, s] = y.astype(jnp.bfloat16)

    def extra_send():
        return remote(help2, g1q.at[1, extra_rows], ex_s, ex_r, (w, r))

    def level1_sends(k):
        n_q = ch if k == 0 else ch - extra
        s = pl.ds(2 * k * ch, n_q)
        to_q = remote(g1z.at[1, s], g1q.at[1, s], l1_s.at[0, k], l1_r.at[0, k], (w, q))
        to_r = remote(help1.at[cut(k)], g1q.at[1, cut(2 * k + 1)], l1_s.at[1, k], l1_r.at[1, k], (w, r))
        return to_q, to_r

    @pl.loop(0, NC)
    def _(k):
        i, j = o_at(k), h_at(k)

        @pl.when(k > 0)
        def _():
            level0_of(h_at(k - 1))

        to_r2, to_q2 = hop2(k)
        to_q2.wait_recv()

        @pl.when(k < NC // 2)
        def _():
            s = cut(j)
            y = trans(part[0, s], foreign(A2_P)) + trans(g2[0, s], cv[2])
            help1[cut(k)] = y.astype(jnp.bfloat16)

        @pl.when(k == NC - 1)
        def _():
            y = trans(part[0, extra_rows], foreign(A2_P)) + trans(g2[0, extra_rows], cv[2])
            help2[...] = y.astype(jnp.bfloat16)

        to_r2.wait_recv()
        level2(1, i)

        for kk in range(NC // 2):
            @pl.when(k == kk)
            def _():
                start(level1_sends(kk))

        @pl.when(k == NC - 1)
        def _():
            extra_send().start()

        level2(0, j)

        @pl.when(k == NC - 1)
        def _():
            pack(CROSS2)
            pack(SELF1)

        level1(0, j)

        @pl.when(k == NC - 1)
        def _():
            scatter(CROSS2)
            scatter(SELF1)

        level0_send(0, j).start()

    level0_of(h_at(NC - 1))

    for k in range(NC // 2):
        s = pair(k)
        to_q, to_r = level1_sends(k)
        ends = k == NC // 2 - 1

        if ends:
            scatter_on(CROSS2)
            scatter_on(SELF1)
            finish_self(SELF2, 2)

        to_q.wait_recv()
        to_r.wait_recv()
        if ends:
            extra_send().wait_recv()
        add(CROSS1, 1, 1, s, g1q)

        if ends:
            pack(CROSS1)

        level1(1, 2 * k)

        if ends:
            scatter(CROSS1)

        level1(1, 2 * k + 1)
        level0_send(1, 2 * k).start()
        level0_send(1, 2 * k + 1).start()
        add(SELF0, 0, 1, s, g0z)

        if ends:
            pack(SELF0)

        level0_send(1, 2 * k).wait_recv()

        if ends:
            scatter(SELF0)

        level0_send(1, 2 * k + 1).wait_recv()
        add(CROSS0, 0, 1, s, g0o)

        if ends:
            pack(CROSS0)

    finish_cross(CROSS2, 2)
    scatter_on(CROSS1)
    scatter(CROSS0)
    last(0)
    finish_self(SELF1, 1)
    scatter_on(SELF0)
    finish_cross(CROSS1, 1)
    last(1)
    scatter_on(CROSS0)
    own_across().start()
    finish_self(SELF0, 0)
    finish(CROSS0, gcv, 0)
    own_across().wait_send()
    for level in (1, 2):
        cross_back(level).wait()

    for c in first_pushes() + second_pushes():
        c.wait_send()
    c0.wait_send()

    @pl.loop(0, NC)
    def _(k):
        for c in hop1(k) + hop2(k) + (level0_send(0, k), level0_send(1, k)):
            c.wait_send()

    for k in range(NC // 2):
        for c in level1_sends(k):
            c.wait_send()
    extra_send().wait_send()

    for i in range(5):
        wait_for(far.at[i, 0, 0, :, left], wy1_s.at[i])
        wait_for(far.at[i, 0, pl.ds(0, WX - 1), :, right], wx1_s.at[i])
        wait_for(far.at[i, :, pl.ds(0, WX - 1), :, left], wx2_s.at[i])
        wait_for(far.at[i, 0, :, :, right], wy2_s.at[i])
    for t in range(6):
        wait_for(got_x.at[t], sx1_s.at[t])
        wait_for(got_y.at[t], sy1_s.at[t])
        wait_for(end_y.at[t], sy2_s.at[t])
        wait_for(end_x.at[t], sx2_s.at[t])


def write_out(outv, gsv, gcv, out_hbm, gs_hbm, gc_hbm, sem):
    n = lax.axis_index("narrow")
    half = outv.shape[1]
    h = lax.rem(lax.div(n, 4), 2)
    copies = []
    for i, (src, dst) in enumerate((
        (outv.at[0], out_hbm.at[pl.ds(pl.multiple_of(h * half, half), half)]),
        (outv.at[1], out_hbm.at[pl.ds(pl.multiple_of((1 - h) * half, half), half)]),
        (gsv, gs_hbm),
        (gcv, gc_hbm),
    )):
        c = pltpu.make_async_copy(src, dst, sem.at[i])
        c.start()
        copies.append(c)
    for c in copies:
        c.wait()


def local(saved_inputs, cotangent, w_self, w_cross):
    wide = lax.axis_size("wide")
    tokens, blk = cotangent.shape
    scale = 1.0 / math.sqrt(tokens * wide)
    half, rows, cols = tokens // 2, blk // wide, blk // 2
    bf, f32 = jnp.bfloat16, jnp.float32
    dma = pltpu.SemaphoreType.DMA
    both = pltpu.VMEM((2, half, blk), bf)
    square3 = pltpu.VMEM((3, blk, blk), bf)

    def body(*refs):
        kernel(wide, scale, *refs)

    vmem, anywhere = pl.BlockSpec(memory_space=pltpu.VMEM), pl.BlockSpec(memory_space=pl.ANY)
    kept = pl.pallas_call(
        body,
        out_shape=(
            pltpu.VMEM((2, half, blk), bf),
            pltpu.VMEM((LEVELS, rows, blk), f32),
            pltpu.VMEM((LEVELS, rows, blk), f32),
        ),
        in_specs=[anywhere] * 4,
        out_specs=[vmem] * 3,
        scratch_shapes=[
            pltpu.VMEM((3, 2, half, blk), bf),
            both,
            square3, square3,
            pltpu.VMEM((5, 2, WX, rows, blk), bf),
            pltpu.VMEM((blk, blk), bf),
            pltpu.VMEM((half, blk), bf), pltpu.VMEM((half, blk), bf),
            both, both, both,
            pltpu.VMEM((half // 2, blk), bf),
            pltpu.VMEM((half // NC // 8, blk), bf),
            both, both,
            pltpu.VMEM((6, blk, blk), f32),
            pltpu.VMEM((6, 2, WX, rows, blk), bf),
            pltpu.VMEM((rows, blk), f32),
            pltpu.VMEM((6, WX - 1, 2, rows, cols), bf),
            pltpu.VMEM((6, WX, rows, cols), bf),
            pltpu.VMEM((6, rows, cols), bf),
            pltpu.VMEM((6, WX, rows, cols), bf),
            pltpu.VMEM((6, rows, blk), f32),
            pltpu.VMEM((WX, rows, cols), f32),
            pltpu.VMEM((6, rows, cols), bf),
            pltpu.VMEM((6, WX - 1, rows, cols), bf),
            pltpu.VMEM((3, rows, blk), f32),
            dma((10,)),
            dma((5,)), dma((5,)),
            *[dma((5,))] * 8,
            dma(()), dma(()),
            dma((2, NC)), dma((2, NC)), dma((2, NC)), dma((2, NC)),
            dma((2, NC // 2)), dma((2, NC // 2)),
            dma((2, NC)), dma((2, NC)),
            *[dma((6,))] * 8,
            dma((3,)), dma((3,)),
            dma(()), dma(()),
            dma(()), dma(()),
        ],
        compiler_params=pltpu.CompilerParams(
            collective_id=0, has_side_effects=True, vmem_limit_bytes=60 << 20
        ),
        name="butterfly_backward",
    )(saved_inputs, cotangent, w_self, w_cross)
    return pl.pallas_call(
        write_out,
        out_shape=(
            jax.ShapeDtypeStruct((tokens, blk), bf),
            jax.ShapeDtypeStruct((LEVELS, rows, blk), f32),
            jax.ShapeDtypeStruct((LEVELS, rows, blk), f32),
        ),
        in_specs=[vmem] * 3,
        out_specs=[anywhere] * 3,
        scratch_shapes=[dma((4,))],
        compiler_params=pltpu.CompilerParams(vmem_limit_bytes=8 << 20),
        name="write_out",
    )(*kept)


def solution(mesh):
    in_specs = (
        P(None, "wide", "narrow"),
        P("wide", "narrow"),
        P(None, "narrow", None),
        P(None, "narrow", None),
    )
    out_specs = (
        P("wide", "narrow"),
        P(None, ("narrow", "wide"), None),
        P(None, ("narrow", "wide"), None),
    )
    return jax.shard_map(local, mesh=mesh, in_specs=in_specs, out_specs=out_specs, check_vma=False)
```
